512 devices in a mesh: seq: 64 (over y, x, core), dp: 8 (over z).
Axes of the slice: x: 4, y: 8, z: 8, core: 2. Of those that a mesh axis runs over, the one named last changes fastest.
Arguments:
- queries: bfloat16 [65536, 1024], P(('dp', 'seq')), parts along dimension 0, may hold values from -6 to 6
- keys: bfloat16 [65536, 1024], P(('dp', 'seq')), parts along dimension 0, may hold values from -4 to 4
- values: bfloat16 [65536, 1024], P(('dp', 'seq')), parts along dimension 0, may hold values from -6 to 6
- cotangent: bfloat16 [65536, 1024], P(('dp', 'seq')), parts along dimension 0, may hold values from -6 to 6
- doc_ids: int32 [65536], P(('dp', 'seq')), parts along dimension 0, may hold values from 0 to 15, never falling along the last dimension, each value on 1 to 4096 neighbouring positions
Outputs:
- attended: bfloat16 [65536, 1024], P(('dp', 'seq')), parts along dimension 0
- grad_queries: bfloat16 [65536, 1024], P(('dp', 'seq')), parts along dimension 0
- grad_keys: bfloat16 [65536, 1024], P(('dp', 'seq')), parts along dimension 0
- grad_values: bfloat16 [65536, 1024], P(('dp', 'seq')), parts along dimension 0
The draws below stay inside these ranges and needn't reach their ends.
There are 8 independent parts, one for each index of `dp`. The reference program is written for one: setup_inputs(seed, part) draws one part's arguments, and reference() takes and returns one part's arrays. A program takes and returns all parts, laid end to end along the dimension named above; each array names one. Nothing has to cross between parts.
Inputs may be any that keep to these rules, and one draw needn't show every extreme that they name: doc_ids never fall along the sequence; each document holds 1 to 4096 positions.
All inputs are finite; a program needn't handle non-finite values.
Results may differ from the reference program's by a relative error of at most 0.0058.
Values may be sent and summed in bfloat16 or wider, within the bound.
A program may use at most 128 MiB of HBM per device.

```python
import math
import jax
import jax.numpy as jnp
import numpy as np
from jax import lax

H = 8
HD = 128
SEG = 1024
LEVELS = 2
SEQ_LEN = 8192
FINEST_DILATION = 4
DOCS = 16
DOC_MOST = 4096


def pair_draw(key):
    shape_full = (SEQ_LEN, H * HD)
    query_base = jax.random.truncated_normal(jax.random.fold_in(key, 11), -4.0, 4.0, shape_full, jnp.float32)
    key_base = jax.random.truncated_normal(jax.random.fold_in(key, 12), -4.0, 4.0, shape_full, jnp.float32)
    return (query_base, key_base)


def draw_queries(key, part):
    return pair_draw(key)[0].astype(jnp.bfloat16)


def draw_keys(key, part):
    return pair_draw(key)[1].astype(jnp.bfloat16)


def block_levels(stream_key, dims, cuts, least, high):
    level = 1.0
    for position, parts in cuts:
        heights = jax.random.uniform(jax.random.fold_in(jax.random.fold_in(stream_key, 6), position), (parts,), jnp.float32, least / len(cuts), high / len(cuts))
        level = level * jnp.repeat(jnp.exp(heights), dims[position] // parts).reshape((-1,) + (1,) * (len(dims) - 1 - position))
    return level


def profile(amount, total, limit, slope):
    loads = [(1 << 20) // math.isqrt(grade ** slope) + 1 for grade in range(2, amount + 1)]
    spare, counts = total - limit - (amount - 1), [1] * (amount - 1)
    while spare > 0:
        free = [i for i in range(amount - 1) if counts[i] < limit]
        pool, left = sum([loads[i] for i in free]), spare
        for i in free:
            more = min(limit - counts[i], max(1, left * loads[i] // pool), spare)
            counts[i] = counts[i] + more
            spare = spare - more
    return np.array([limit] + counts)


def ragged_sizes(own_key, amount, total, bound, lean):
    if amount == 2:
        one = jax.random.randint(own_key, (), max(1, total - bound), min(bound, total - 1) + 1)
        return jnp.stack([one, total - one])
    lengths = jnp.asarray(profile(amount, total, bound, lean), jnp.int32)
    pairs = (amount - 1) // 2
    source_of, taker = lengths[1:1 + 2 * pairs:2], lengths[2:2 + 2 * pairs:2]
    slack = jnp.minimum(source_of - 1, bound - taker)
    passed = jax.random.randint(jax.random.fold_in(own_key, 1), (pairs,), 0, 1 << 20) % (slack + 1)
    lengths = lengths.at[1:1 + 2 * pairs:2].set(source_of - passed).at[2:2 + 2 * pairs:2].set(taker + passed)
    return lengths[jax.random.permutation(jax.random.fold_in(own_key, 2), amount)]


def bell_draw(own_key, shape, scale, limit, split=(), kind=jnp.bfloat16):
    values = scale * jax.random.normal(own_key, shape, jnp.float32)
    if split:
        values = values * block_levels(own_key, shape, split, -0.22, 0.18)
    return jnp.clip(values, -limit, limit).astype(kind)


def setup_inputs(seed: int = 0, part: int = 0) -> dict:
    key_of = jax.random.split(jax.random.key(seed), 6)
    part_splits = jax.random.split(jax.random.fold_in(key_of[5], part), 6)
    queries = draw_queries(jax.random.fold_in(jax.random.fold_in(key_of[5], part), 71), part)
    keys = draw_keys(jax.random.fold_in(jax.random.fold_in(key_of[5], part), 71), part)
    values = bell_draw(part_splits[2], (SEQ_LEN, H * HD), 1.0, 6.0, ((0, 64),))
    cotangent = bell_draw(part_splits[3], (SEQ_LEN, H * HD), 1.0, 6.0, ((0, 64),))
    doc_ids = jnp.searchsorted(jnp.cumsum(ragged_sizes(part_splits[4], DOCS, SEQ_LEN, DOC_MOST, 2)), jnp.arange(SEQ_LEN), side="right").astype(jnp.int32)
    return {"queries": queries, "keys": keys, "values": values, "cotangent": cotangent, "doc_ids": doc_ids}


MASKED = -1e30


def dilate(array, dilation_step):
    heads = array.shape[1]
    rows = array.shape[0] // dilation_step
    shaped = array.reshape((rows, dilation_step) + array.shape[1:])
    return shaped[:, np.arange(heads) % dilation_step, np.arange(heads)]


def place_rows(array, dilation_step, filler):
    heads = array.shape[1]
    rows = array.shape[0]
    empty = jnp.full((rows, dilation_step) + array.shape[1:], filler, array.dtype)
    filled = empty.at[:, np.arange(heads) % dilation_step, np.arange(heads)].set(array)
    return filled.reshape((rows * dilation_step,) + array.shape[1:])


def coarsen(array):
    return lax.optimization_barrier(array.astype(jnp.bfloat16)).astype(jnp.float32)


def score_block(query_seg, key_segment, doc_seg):
    index = jnp.arange(query_seg.shape[0])
    allowed = (index[None, :] <= index[:, None])[None] & (doc_seg.T[:, :, None] == doc_seg.T[:, None, :])
    score = jnp.einsum("ihd,jhd->hij", query_seg, key_segment, precision=lax.Precision.HIGHEST) * (HD ** -0.5)
    return jnp.where(allowed, score, MASKED)


def segment_forward(item):
    query_seg, key_segment, value_seg, doc_seg = item
    score = score_block(query_seg, key_segment, doc_seg)
    top_score = jnp.max(score, -1)
    log_total = top_score + jnp.log(jnp.sum(jnp.exp(score - top_score[..., None]), -1))
    probs = jnp.exp(score - log_total[..., None])
    attended = jnp.einsum("hij,jhd->ihd", coarsen(probs), value_seg, precision=lax.Precision.HIGHEST)
    return log_total, attended


def segment_backward(item):
    query_seg, key_segment, value_seg, dout_seg, doc_seg, log_total, gain_segment, dot_seg = item
    highest = lax.Precision.HIGHEST
    probs = jnp.exp(score_block(query_seg, key_segment, doc_seg) - log_total[..., None])
    dprob = jnp.einsum("ihd,jhd->hij", dout_seg, value_seg, precision=highest)
    gain = gain_segment.T[:, :, None]
    dscore = coarsen(gain * probs * (dprob - dot_seg.T[:, :, None]))
    weighted = coarsen(gain * probs)
    level_queries = jnp.einsum("hij,jhd->ihd", dscore, key_segment, precision=highest) * (HD ** -0.5)
    level_k = jnp.einsum("hij,ihd->jhd", dscore, query_seg, precision=highest) * (HD ** -0.5)
    level_v = jnp.einsum("hij,ihd->jhd", weighted, dout_seg, precision=highest)
    return level_queries, level_k, level_v


def reference(queries, keys, values, cotangent, doc_ids):
    length_all = queries.shape[0]
    query_rows = queries.reshape(length_all, H, HD)
    key_rows = keys.reshape(length_all, H, HD)
    value_rows = values.reshape(length_all, H, HD)
    grad_rows = cotangent.reshape(length_all, H, HD)
    doc_heads = jnp.broadcast_to(doc_ids[:, None], (length_all, H))

    def segment_cut(array, dilation_step):
        segments = length_all // (SEG * dilation_step)
        return dilate(array, dilation_step).reshape((segments, SEG) + array.shape[1:])

    lse_full = []
    part_full = []
    lse_saved = []
    for index_of_level in range(LEVELS):
        dilation_step = FINEST_DILATION * 2 ** index_of_level
        inputs = (segment_cut(query_rows, dilation_step).astype(jnp.float32),
                  segment_cut(key_rows, dilation_step).astype(jnp.float32),
                  segment_cut(value_rows, dilation_step).astype(jnp.float32),
                  segment_cut(doc_heads, dilation_step))
        log_total, attended = lax.map(segment_forward, inputs)
        lse_full.append(place_rows(log_total.transpose(0, 2, 1).reshape(-1, H), dilation_step, MASKED))
        part_full.append(place_rows(attended.reshape(-1, H, HD), dilation_step, 0.0))
        lse_saved.append(log_total)
    top_level = lse_full[0]
    for index_of_level in range(1, LEVELS):
        top_level = jnp.maximum(top_level, lse_full[index_of_level])
    level_total = jnp.zeros_like(top_level)
    for index_of_level in range(LEVELS):
        level_total = level_total + jnp.exp(lse_full[index_of_level] - top_level)
    merged_log = top_level + jnp.log(level_total)
    weight_matrix = [jnp.exp(entry_lse - merged_log) for entry_lse in lse_full]
    combined = jnp.zeros((length_all, H, HD), jnp.float32)
    for index_of_level in range(LEVELS):
        combined = combined + weight_matrix[index_of_level][..., None] * part_full[index_of_level]
    dot_sum = jnp.sum(grad_rows.astype(jnp.float32) * combined, -1)
    grad_query = jnp.zeros((length_all, H, HD), jnp.float32)
    grad_key = jnp.zeros((length_all, H, HD), jnp.float32)
    grad_value = jnp.zeros((length_all, H, HD), jnp.float32)
    for index_of_level in range(LEVELS):
        dilation_step = FINEST_DILATION * 2 ** index_of_level
        inputs = (segment_cut(query_rows, dilation_step).astype(jnp.float32),
                  segment_cut(key_rows, dilation_step).astype(jnp.float32),
                  segment_cut(value_rows, dilation_step).astype(jnp.float32),
                  segment_cut(grad_rows, dilation_step).astype(jnp.float32),
                  segment_cut(doc_heads, dilation_step),
                  lse_saved[index_of_level],
                  segment_cut(weight_matrix[index_of_level], dilation_step),
                  segment_cut(dot_sum, dilation_step))
        level_queries, level_k, level_v = lax.map(segment_backward, inputs)
        grad_query = grad_query + place_rows(level_queries.reshape(-1, H, HD), dilation_step, 0.0)
        grad_key = grad_key + place_rows(level_k.reshape(-1, H, HD), dilation_step, 0.0)
        grad_value = grad_value + place_rows(level_v.reshape(-1, H, HD), dilation_step, 0.0)
    flattened_shape = (length_all, H * HD)
    return (combined.astype(jnp.bfloat16).reshape(flattened_shape),
            grad_query.astype(jnp.bfloat16).reshape(flattened_shape),
            grad_key.astype(jnp.bfloat16).reshape(flattened_shape),
            grad_value.astype(jnp.bfloat16).reshape(flattened_shape))
```

```python
import jax
import jax.numpy as jnp
from jax import lax
from jax.experimental import pallas as pl
from jax.experimental.pallas import tpu as pltpu
from jax.sharding import PartitionSpec as P

H = 8
HD = 128
SEQ_DEVICES = 64
GROUP = 32
TOKENS = 128
ROWS = 16
SEG_ROWS = GROUP * ROWS
BLOCK = 256
CLASSES = 8
FINEST = 4
SCORE_SCALE = HD**-0.5
LOG2_E = 1.4426950408889634
MASKED = -1e30
MESH_ID = pl.DeviceIdType.MESH

Q_A, Q_B, K_B, V_B, D_A, D_B, K_A, V_A, DOC = range(9)
Q_OF, K_OF, V_OF, D_OF = (Q_A, Q_B), (K_A, K_B), (V_A, V_B), (D_A, D_B)


def dot_nn(a, b):
    return jnp.dot(a, b, preferred_element_type=jnp.float32)


def dot_nt(a, b):
    return lax.dot_general(a, b, (((1,), (1,)), ((), ())), preferred_element_type=jnp.float32)


def iota(shape, dim):
    return lax.broadcasted_iota(jnp.int32, shape, dim)


def one_hot_rows(shape, lane):
    return (iota(shape, 1) == lane).astype(jnp.bfloat16)


def selector(head):
    shape = (2 * ROWS, TOKENS)
    row = iota(shape, 0)
    kind = (head + FINEST * (row >> 4)) & (CLASSES - 1)
    return iota(shape, 1) == CLASSES * (row & (ROWS - 1)) + kind


def worker_of(head, half):
    return GROUP * half + 8 + 2 * head


def exchange_kernel(
    q_hbm, k_hbm, v_hbm, g_hbm, doc_ref, back, backx,
    xin, snd, recv, recvx, res, resx, col, row, kt, vt, sbuf, dpbuf, dkv,
    in_sem, send_sem, recv_sem, recvx_sem, ret_sem, back_sem, backx_sem,
):
    me = lax.axis_index("seq")
    half = me // GROUP
    rank = lax.rem(me, GROUP)
    is_worker = (rank >= 8) & (rank < 24) & (lax.rem(rank, 2) == 0)
    head = (rank - 8) // 2

    loads = [
        pltpu.make_async_copy(ref, xin.at[i], in_sem.at[i])
        for i, ref in enumerate((q_hbm, k_hbm, v_hbm, g_hbm))
    ]
    for load in loads:
        load.start()

    barrier = pltpu.get_barrier_semaphore()

    def greet(device):
        @pl.when(device != me)
        def _():
            pl.semaphore_signal(barrier, inc=1, device_id={"seq": device}, device_id_type=MESH_ID)

    @pl.when(half == 0)
    def _():
        lax.fori_loop(0, H, lambda i, c: (greet(worker_of(i, 0)), c)[1], 0)

    lax.fori_loop(0, H, lambda i, c: (greet(worker_of(i, 1)), c)[1], 0)

    @pl.when(is_worker)
    def _():
        lax.fori_loop(0, GROUP * (1 + half), lambda i, c: (greet(i), c)[1], 0)

    packs = [selector(h) for h in range(H)]
    doc_row = jnp.broadcast_to(doc_ref[...], (2 * ROWS, TOKENS)).astype(jnp.float32)
    ones = jnp.ones((TOKENS, TOKENS), jnp.bfloat16)
    first_lanes = iota((ROWS, HD), 1) < HD // 2
    for h in range(H):
        docs = dot_nn(jnp.where(packs[h], doc_row, 0.0).astype(jnp.bfloat16), ones)
        snd[h, DOC] = jnp.where(first_lanes, docs[:ROWS], docs[ROWS:]).astype(jnp.bfloat16)
    one_hots = [p.astype(jnp.bfloat16) for p in packs]
    for i, (slot_a, slot_b) in enumerate(((Q_A, Q_B), (K_A, K_B), (V_A, V_B), (D_A, D_B))):
        loads[i].wait()
        for h in range(H):
            rows = dot_nn(one_hots[h], xin[i, :, h * HD : (h + 1) * HD]).astype(jnp.bfloat16)
            snd[h, slot_a] = rows[:ROWS]
            snd[h, slot_b] = rows[ROWS:]

    own_sources = jnp.where(is_worker, GROUP * (1 + half) - 1, 0)
    own_workers = jnp.where(half == 0, 2 * H, H) - jnp.where(is_worker, 1, 0)
    pl.semaphore_wait(barrier, own_sources + own_workers)

    place = pl.ds(pl.multiple_of(rank * ROWS, ROWS), ROWS)

    def send_main(h):
        return pltpu.make_async_remote_copy(
            snd.at[h], recv.at[:, place], send_sem, recv_sem,
            device_id={"seq": worker_of(h, half)}, device_id_type=MESH_ID,
        )

    def send_cross(h):
        return pltpu.make_async_remote_copy(
            snd.at[h, pl.ds(K_A, 3)], recvx.at[:, place], send_sem, recvx_sem,
            device_id={"seq": worker_of(h, 1)}, device_id_type=MESH_ID,
        )

    def send_head(i, carry):
        h = lax.rem(i + me, H)
        target = worker_of(h, half)

        @pl.when(target != me)
        def _():
            send_main(h).start()

        @pl.when(target == me)
        def _():
            pltpu.make_async_copy(snd.at[h], recv.at[:, place], recv_sem).start()

        @pl.when(half == 0)
        def _():
            send_cross(h).start()

        return carry

    lax.fori_loop(0, H, send_head, 0)

    @pl.when(is_worker)
    def _():
        @pl.when(half == 0)
        def _():
            recvx[...] = jnp.zeros_like(recvx)

        pltpu.make_async_copy(recv, recv, recv_sem).wait()

        @pl.when(half == 1)
        def _():
            pltpu.make_async_copy(recvx, recvx, recvx_sem).wait()

        attention(head, half, recv, recvx, res, resx, col, row, kt, vt, sbuf, dpbuf, dkv)

        def send_back(i, carry):
            r = lax.rem(i + rank, GROUP)
            target = GROUP * half + r
            rows = pl.ds(pl.multiple_of(r * ROWS, ROWS), ROWS)

            @pl.when(target != me)
            def _():
                pltpu.make_async_remote_copy(
                    res.at[:, rows], back.at[head], ret_sem, back_sem,
                    device_id={"seq": target}, device_id_type=MESH_ID,
                ).start()

            @pl.when(target == me)
            def _():
                pltpu.make_async_copy(res.at[:, rows], back.at[head], back_sem).start()

            @pl.when(half == 1)
            def _():
                pltpu.make_async_remote_copy(
                    resx.at[:, rows], backx.at[head], ret_sem, backx_sem,
                    device_id={"seq": r}, device_id_type=MESH_ID,
                ).start()

            return carry

        lax.fori_loop(0, GROUP, send_back, 0)

    pltpu.make_async_copy(back, back, back_sem).wait()

    @pl.when(half == 0)
    def _():
        pltpu.make_async_copy(backx, backx, backx_sem).wait()

    def sent_head(h, carry):
        @pl.when(worker_of(h, half) != me)
        def _():
            send_main(h).wait_send()

        @pl.when(half == 0)
        def _():
            send_cross(h).wait_send()

        return carry

    lax.fori_loop(0, H, sent_head, 0)

    @pl.when(is_worker)
    def _():
        def sent_back(i, carry):
            @pl.when(GROUP * half + i != me)
            def _():
                pltpu.make_async_remote_copy(
                    res.at[:, pl.ds(0, ROWS)], back.at[head], ret_sem, back_sem,
                    device_id={"seq": i}, device_id_type=MESH_ID,
                ).wait_send()

            @pl.when(half == 1)
            def _():
                pltpu.make_async_remote_copy(
                    resx.at[:, pl.ds(0, ROWS)], backx.at[head], ret_sem, backx_sem,
                    device_id={"seq": i}, device_id_type=MESH_ID,
                ).wait_send()

            return carry

        lax.fori_loop(0, GROUP, sent_back, 0)


def attention(head, half, recv, recvx, res, resx, col, row, kt, vt, sbuf, dpbuf, dkv):
    eye = (iota((HD, HD), 0) == iota((HD, HD), 1)).astype(jnp.bfloat16)
    eye_block = (iota((BLOCK, BLOCK), 0) == iota((BLOCK, BLOCK), 1)).astype(jnp.bfloat16)
    pick_a = (iota((HD, HD), 0) == 0).astype(jnp.bfloat16)
    pick_b = (iota((HD, HD), 0) == HD // 2).astype(jnp.bfloat16)
    key_refs = [(recv.at[K_A], recv.at[V_A]), (recv.at[K_B], recv.at[V_B]), (recvx.at[0], recvx.at[1])]
    for g, (k_ref, v_ref) in enumerate(key_refs):
        kt[g] = dot_nt(eye, k_ref[...]).astype(jnp.bfloat16)
        vt[g] = dot_nt(eye, v_ref[...]).astype(jnp.bfloat16)
    docs = recv[DOC]
    col[0] = dot_nn(docs, pick_a)
    col[1] = dot_nn(docs, pick_b)
    col[2] = jnp.where(half == 1, dot_nn(recvx[2], pick_a), -1.0)
    row[0] = dot_nt(one_hot_rows((8, HD), 0), docs)
    row[1] = dot_nt(one_hot_rows((8, HD), HD // 2), docs)

    lower = iota((BLOCK, BLOCK), 0) - iota((BLOCK, BLOCK), 1)
    b_is_later = jnp.where(head < FINEST, 1, 0)
    most = {(0, 0): 0, (1, 1): 0, (0, 1): -b_is_later, (1, 0): b_is_later - 1}
    started = set()
    for kind in (0, 1):
        for b in (0, 1):
            own = pl.ds(b * BLOCK, BLOCK)
            q = recv[Q_OF[kind], own]
            g = recv[D_OF[kind], own]
            q_docs = row[kind, 0:1, own]
            tiles = [(group, t) for group in (0, 1) for t in range(b + 1)]
            if kind == 0:
                tiles += [(2, 0), (2, 1)]
            top = None
            for n, (group, t) in enumerate(tiles):
                rows = pl.ds(t * BLOCK, BLOCK)
                s = dot_nt(key_refs[group][0][rows], q) * (SCORE_SCALE * LOG2_E)
                if kind == 0 and group == 0:
                    s = s + 1.0
                k_docs = col[group, rows]
                allowed = jnp.concatenate([k_docs, k_docs], 1) == q_docs
                if group < 2 and t == b:
                    allowed = allowed & (lower <= most[(kind, group)])
                s = jnp.where(allowed, s, MASKED)
                sbuf[n] = s
                tile_top = jnp.max(s, 0, keepdims=True)
                top = tile_top if top is None else jnp.maximum(top, tile_top)
            total = jnp.zeros((1, BLOCK), jnp.float32)
            drop = jnp.zeros((1, BLOCK), jnp.float32)
            for n, (group, t) in enumerate(tiles):
                rows = pl.ds(t * BLOCK, BLOCK)
                e = jnp.exp2(sbuf[n] - top)
                dp = dot_nt(key_refs[group][1][rows], g)
                total = total + jnp.sum(e, 0, keepdims=True)
                drop = drop + jnp.sum(e * dp, 0, keepdims=True)
                sbuf[n] = e
                dpbuf[n] = dp
            inverse = 1.0 / total
            drop = drop * inverse
            out_t = jnp.zeros((HD, BLOCK), jnp.float32)
            dq_t = jnp.zeros((HD, BLOCK), jnp.float32)
            for n, (group, t) in enumerate(tiles):
                rows = pl.ds(t * BLOCK, BLOCK)
                w = sbuf[n] * inverse
                ds = (w * (dpbuf[n] - drop)).astype(jnp.bfloat16)
                w = w.astype(jnp.bfloat16)
                out_t = out_t + dot_nn(vt[group, :, rows], w)
                dq_t = dq_t + dot_nn(kt[group, :, rows], ds)
                dk = dot_nn(ds, q)
                dv = dot_nn(w, g)
                if (group, t) in started:
                    dk = dk + dkv[0, group, rows]
                    dv = dv + dkv[1, group, rows]
                started.add((group, t))
                dkv[0, group, rows] = dk
                dkv[1, group, rows] = dv
            res[kind, own] = dot_nt(eye_block, out_t.astype(jnp.bfloat16)).astype(jnp.bfloat16)
            dq = (dq_t * SCORE_SCALE).astype(jnp.bfloat16)
            res[2 + kind, own] = dot_nt(eye_block, dq).astype(jnp.bfloat16)
    for kind in (0, 1):
        res[4 + kind] = (dkv[0, kind] * SCORE_SCALE).astype(jnp.bfloat16)
        res[6 + kind] = dkv[1, kind].astype(jnp.bfloat16)
    resx[0] = (dkv[0, 2] * SCORE_SCALE).astype(jnp.bfloat16)
    resx[1] = dkv[1, 2].astype(jnp.bfloat16)


def place_kernel(back, backx, o_ref, dq_ref, dk_ref, dv_ref):
    first = lax.axis_index("seq") < GROUP
    for h in range(H):
        shape = (TOKENS, 2 * ROWS)
        rank = iota(shape, 1)
        kind = (h + FINEST * (rank >> 4)) & (CLASSES - 1)
        spread = (iota(shape, 0) == CLASSES * (rank & (ROWS - 1)) + kind).astype(jnp.bfloat16)
        lanes = pl.ds(h * HD, HD)
        for i, ref in enumerate((o_ref, dq_ref, dk_ref, dv_ref)):
            rows = back[h, 2 * i : 2 * i + 2].reshape(2 * ROWS, HD)
            if i >= 2:
                extra = jnp.where(first, backx[h, i - 2].astype(jnp.float32), 0.0)
                summed = (back[h, 2 * i].astype(jnp.float32) + extra).astype(jnp.bfloat16)
                rows = jnp.concatenate([summed, back[h, 2 * i + 1]], 0)
            ref[:, lanes] = dot_nn(spread, rows).astype(jnp.bfloat16)


def per_device(queries, keys, values, cotangent, doc_ids):
    any_space = pl.BlockSpec(memory_space=pl.ANY)
    vmem = pl.BlockSpec(memory_space=pltpu.VMEM)
    bf16, f32 = jnp.bfloat16, jnp.float32
    dma = pltpu.SemaphoreType.DMA
    back, backx = pl.pallas_call(
        exchange_kernel,
        out_shape=(
            jax.ShapeDtypeStruct((H, 8, ROWS, HD), bf16),
            jax.ShapeDtypeStruct((H, 2, ROWS, HD), bf16),
        ),
        in_specs=[any_space] * 4 + [vmem],
        out_specs=(any_space, any_space),
        scratch_shapes=[
            pltpu.VMEM((4, TOKENS, H * HD), bf16),
            pltpu.VMEM((H, 9, ROWS, HD), bf16),
            pltpu.VMEM((9, SEG_ROWS, HD), bf16),
            pltpu.VMEM((3, SEG_ROWS, HD), bf16),
            pltpu.VMEM((8, SEG_ROWS, HD), bf16),
            pltpu.VMEM((2, SEG_ROWS, HD), bf16),
            pltpu.VMEM((3, SEG_ROWS, HD), f32),
            pltpu.VMEM((2, 8, SEG_ROWS), f32),
            pltpu.VMEM((3, HD, SEG_ROWS), bf16),
            pltpu.VMEM((3, HD, SEG_ROWS), bf16),
            pltpu.VMEM((6, BLOCK, BLOCK), f32),
            pltpu.VMEM((6, BLOCK, BLOCK), f32),
            pltpu.VMEM((2, 3, SEG_ROWS, HD), f32),
            dma((4,)),
            dma,
            dma,
            dma,
            dma,
            dma,
            dma,
        ],
        compiler_params=pltpu.CompilerParams(
            collective_id=0, has_side_effects=True, vmem_limit_bytes=48 * 2**20
        ),
        name="exchange",
    )(queries, keys, values, cotangent, doc_ids.reshape(1, TOKENS))
    full = jax.ShapeDtypeStruct((TOKENS, H * HD), bf16)
    return tuple(
        pl.pallas_call(
            place_kernel,
            out_shape=(full,) * 4,
            in_specs=[vmem, vmem],
            out_specs=(vmem,) * 4,
            name="place",
        )(back, backx)
    )


def solution(mesh):
    spec = P(("dp", "seq"), None)
    return jax.shard_map(
        per_device,
        mesh=mesh,
        in_specs=(spec, spec, spec, spec, P(("dp", "seq"))),
        out_specs=(spec,) * 4,
        check_vma=False,
    )
```

```python
import jax
import jax.numpy as jnp
from jax import lax
from jax.experimental import pallas as pl
from jax.experimental.pallas import tpu as pltpu
from jax.sharding import PartitionSpec as P

H = 8
HD = 128
SEQ_DEVICES = 64
GROUP = 32
TOKENS = 128
ROWS = 16
SEG_ROWS = GROUP * ROWS
BLOCK = 256
CLASSES = 8
FINEST = 4
SCORE_SCALE = HD**-0.5
LOG2_E = 1.4426950408889634
MASKED = -1e30
MESH_ID = pl.DeviceIdType.MESH

MESSAGE = 8 * ROWS + 8
CROSS_AT = 6 * ROWS
CROSS = MESSAGE - CROSS_AT

Q_OF, K_OF, V_OF, D_OF = (0, 1), (6, 4), (7, 5), (2, 3)


def dot_nn(a, b):
    return jnp.dot(a, b, preferred_element_type=jnp.float32)


def dot_nt(a, b):
    return lax.dot_general(a, b, (((1,), (1,)), ((), ())), preferred_element_type=jnp.float32)


def iota(shape, dim):
    return lax.broadcasted_iota(jnp.int32, shape, dim)


def selector(head):
    shape = (2 * ROWS, TOKENS)
    row = iota(shape, 0)
    kind = (head + FINEST * (row >> 4)) & (CLASSES - 1)
    return iota(shape, 1) == CLASSES * (row & (ROWS - 1)) + kind


def worker_of(head, half):
    return GROUP * half + 8 + 2 * head


def exchange_kernel(
    q_hbm, k_hbm, v_hbm, g_hbm, doc_ref, back, backx,
    xin, snd, recv, recvx, res, resx, kt, vt, s0, dp0, e_own, dp_own, stat, ot0, dqt0, dkv,
    in_sem, send_sem, recv_sem, recvx_sem, ret_sem, back_sem, backx_sem,
):
    me = lax.axis_index("seq")
    half = me // GROUP
    rank = lax.rem(me, GROUP)
    is_worker = (rank >= 8) & (rank < 24) & (lax.rem(rank, 2) == 0)
    head = (rank - 8) // 2

    loads = [
        pltpu.make_async_copy(ref, xin.at[i], in_sem.at[i])
        for i, ref in enumerate((q_hbm, k_hbm, v_hbm, g_hbm))
    ]
    for load in loads:
        load.start()

    barrier = pltpu.get_barrier_semaphore()

    def greet(device):
        @pl.when(device != me)
        def _():
            pl.semaphore_signal(barrier, inc=1, device_id={"seq": device}, device_id_type=MESH_ID)

    @pl.when(half == 0)
    def _():
        lax.fori_loop(0, H, lambda i, c: (greet(worker_of(i, 0)), c)[1], 0)

    lax.fori_loop(0, H, lambda i, c: (greet(worker_of(i, 1)), c)[1], 0)

    @pl.when(is_worker)
    def _():
        lax.fori_loop(0, GROUP * (1 + half), lambda i, c: (greet(i), c)[1], 0)

    docs = jnp.broadcast_to(doc_ref[...].astype(jnp.float32), (8, TOKENS)).astype(jnp.bfloat16)
    for h in range(H):
        snd[h, 8 * ROWS : MESSAGE] = docs
    one_hots = [selector(h).astype(jnp.bfloat16) for h in range(H)]
    for i, slots in enumerate((Q_OF, K_OF, V_OF, D_OF)):
        loads[i].wait()
        for h in range(H):
            rows = dot_nn(one_hots[h], xin[i, :, h * HD : (h + 1) * HD]).astype(jnp.bfloat16)
            for kind, slot in enumerate(slots):
                snd[h, slot * ROWS : (slot + 1) * ROWS] = rows[kind * ROWS : (kind + 1) * ROWS]

    own_sources = jnp.where(is_worker, GROUP * (1 + half) - 1, 0)
    own_workers = jnp.where(half == 0, 2 * H, H) - jnp.where(is_worker, 1, 0)
    pl.semaphore_wait(barrier, own_sources + own_workers)


    def send_main(h):
        return pltpu.make_async_remote_copy(
            snd.at[h], recv.at[rank], send_sem, recv_sem,
            device_id={"seq": worker_of(h, half)}, device_id_type=MESH_ID,
        )

    def send_cross(h):
        return pltpu.make_async_remote_copy(
            snd.at[h, pl.ds(CROSS_AT, CROSS)], recvx.at[rank], send_sem, recvx_sem,
            device_id={"seq": worker_of(h, 1)}, device_id_type=MESH_ID,
        )

    def send_head(i, carry):
        h = lax.rem(i + me, H)
        target = worker_of(h, half)

        @pl.when(target != me)
        def _():
            send_main(h).start()

        @pl.when(target == me)
        def _():
            pltpu.make_async_copy(snd.at[h], recv.at[rank], recv_sem).start()

        return carry

    def send_cross_head(i, carry):
        send_cross(lax.rem(i + me, H)).start()
        return carry

    @pl.when(half == 0)
    def _():
        lax.fori_loop(0, H, send_cross_head, 0)

    lax.fori_loop(0, H, send_head, 0)

    @pl.when(is_worker)
    def _():
        pltpu.make_async_copy(recv, recv, recv_sem).wait()

        @pl.when(half == 1)
        def _():
            pltpu.make_async_copy(recvx, recvx, recvx_sem).wait()

        def send_cross_back(i, carry):
            r = lax.rem(i + rank, GROUP)
            pltpu.make_async_remote_copy(
                resx.at[r], backx.at[head], ret_sem, backx_sem,
                device_id={"seq": r}, device_id_type=MESH_ID,
            ).start()
            return carry

        def send_back(block):
            def one(i, carry):
                r = block * 8 + lax.rem(i + rank, 8)
                target = GROUP * half + r

                @pl.when(target != me)
                def _():
                    pltpu.make_async_remote_copy(
                        res.at[r], back.at[head], ret_sem, back_sem,
                        device_id={"seq": target}, device_id_type=MESH_ID,
                    ).start()

                @pl.when(target == me)
                def _():
                    pltpu.make_async_copy(res.at[r], back.at[head], back_sem).start()

                return carry

            lax.fori_loop(0, 8, one, 0)

        def send_crosses():
            lax.fori_loop(0, GROUP, send_cross_back, 0)

        attention(
            head, half, recv, recvx, res, resx, kt, vt, s0, dp0, e_own, dp_own, stat, ot0, dqt0, dkv,
            send_crosses, send_back,
        )

    pltpu.make_async_copy(back, back, back_sem).wait()

    @pl.when(half == 0)
    def _():
        pltpu.make_async_copy(backx, backx, backx_sem).wait()

    def sent_head(h, carry):
        @pl.when(worker_of(h, half) != me)
        def _():
            send_main(h).wait_send()

        @pl.when(half == 0)
        def _():
            send_cross(h).wait_send()

        return carry

    lax.fori_loop(0, H, sent_head, 0)

    @pl.when(is_worker)
    def _():
        def sent_back(i, carry):
            @pl.when(GROUP * half + i != me)
            def _():
                pltpu.make_async_remote_copy(
                    res.at[i], back.at[head], ret_sem, back_sem,
                    device_id={"seq": i}, device_id_type=MESH_ID,
                ).wait_send()

            @pl.when(half == 1)
            def _():
                pltpu.make_async_remote_copy(
                    resx.at[i], backx.at[head], ret_sem, backx_sem,
                    device_id={"seq": i}, device_id_type=MESH_ID,
                ).wait_send()

            return carry

        lax.fori_loop(0, GROUP, sent_back, 0)


def tile_rows(ref, tile):
    return ref[:, tile * ROWS : (tile + 1) * ROWS].reshape(SEG_ROWS, HD)


def class_docs(ref, at, kind):
    eight = ref[:, at : at + 8].astype(jnp.float32)
    spread = jnp.concatenate([eight, eight], 1).reshape(SEG_ROWS, HD)
    shape = (SEG_ROWS, HD)
    own = iota(shape, 1) == CLASSES * (iota(shape, 0) & (ROWS - 1)) + kind
    picked = jnp.where(own, spread, 0.0).astype(jnp.bfloat16)
    ones = jnp.ones((HD, HD), jnp.bfloat16)
    return dot_nn(picked, ones), dot_nt(ones[:8], picked)


def attention(
    head, half, recv, recvx, res, resx, kt, vt, s0, dp0, e_own, dp_own, stat, ot0, dqt0, dkv,
    send_crosses, send_back,
):
    bf16, f32 = jnp.bfloat16, jnp.float32
    scale = SCORE_SCALE * LOG2_E
    eye = (iota((HD, HD), 0) == iota((HD, HD), 1)).astype(bf16)
    eye_block = (iota((BLOCK, BLOCK), 0) == iota((BLOCK, BLOCK), 1)).astype(bf16)
    q_all = [tile_rows(recv, t) for t in Q_OF]
    k_all = [tile_rows(recv, t) for t in K_OF]
    v_all = [tile_rows(recv, t) for t in V_OF]
    g_all = [tile_rows(recv, t) for t in D_OF]
    for kind in (0, 1):
        kt[kind] = dot_nt(eye, k_all[kind]).astype(bf16)
        vt[kind] = dot_nt(eye, v_all[kind]).astype(bf16)
    docs = [class_docs(recv, 8 * ROWS, (head + FINEST * kind) & (CLASSES - 1)) for kind in (0, 1)]
    cols = [d[0] for d in docs]
    q_docs = [d[1][0:1] for d in docs]

    stat[0] = jnp.full((8, SEG_ROWS), MASKED, f32)
    stat[1] = jnp.zeros((8, SEG_ROWS), f32)
    stat[2] = jnp.zeros((8, SEG_ROWS), f32)
    ot0[...] = jnp.zeros_like(ot0)
    dqt0[...] = jnp.zeros_like(dqt0)

    @pl.when(half == 1)
    def _():
        col0, _ = class_docs(recvx, 2 * ROWS, head)
        k0 = tile_rows(recvx, 0)
        kt[2] = dot_nt(eye, k0).astype(bf16)
        vt[2] = dot_nt(eye, tile_rows(recvx, 1)).astype(bf16)
        for c in range(0, SEG_ROWS, BLOCK):
            at = pl.ds(c, BLOCK)
            query = q_all[0][c : c + BLOCK]
            top = None
            for r in range(0, SEG_ROWS, BLOCK):
                doc = col0[r : r + BLOCK]
                s = dot_nt(k0[r : r + BLOCK], query) * scale
                allowed = jnp.concatenate([doc, doc], 1) == q_docs[0][:, c : c + BLOCK]
                s = jnp.where(allowed, s, MASKED)
                s0[pl.ds(r, BLOCK), at] = s
                t = jnp.max(s, 0, keepdims=True)
                top = t if top is None else jnp.maximum(top, t)
            stat[0, 0:1, at] = top

    lower = iota((HD, BLOCK), 0) - (iota((HD, BLOCK), 1) & (HD - 1))
    is_a = iota((HD, BLOCK), 1) < HD
    b_is_later = jnp.where(head < FINEST, 1, 0)
    in_order = [
        lower <= jnp.where(is_a, 0, b_is_later - 1),
        lower <= jnp.where(is_a, -b_is_later, 0),
    ]
    bonus = jnp.where(iota((1, BLOCK), 1) < HD, 1.0, 0.0)
    both = lambda pair, i: jnp.concatenate([pair[0][i * HD : (i + 1) * HD], pair[1][i * HD : (i + 1) * HD]], 0)
    lanes = lambda pair, i: jnp.concatenate([pair[0][:, i * HD : (i + 1) * HD], pair[1][:, i * HD : (i + 1) * HD]], 1)
    blocks = SEG_ROWS // HD
    qs = [both(q_all, i) for i in range(blocks)]
    gs = [both(g_all, i) for i in range(blocks)]
    totals, drops = [], []
    for i in range(blocks):
        query_docs = lanes(q_docs, i)
        at = pl.ds(i * HD, HD)
        top = jnp.concatenate([stat[0, 0:1, at], jnp.full((1, HD), MASKED, f32)], 1)
        for kind in (0, 1):
            for t in range(i + 1):
                rows = slice(t * HD, (t + 1) * HD)
                s = dot_nt(k_all[kind][rows], qs[i]) * scale
                if kind == 0:
                    s = s + bonus
                doc = cols[kind][rows]
                allowed = jnp.concatenate([doc, doc], 1) == query_docs
                if t == i:
                    allowed = allowed & in_order[kind]
                s = jnp.where(allowed, s, MASKED)
                e_own[i, kind, rows] = s
                top = jnp.maximum(top, jnp.max(s, 0, keepdims=True))
        stat[0, 0:1, at] = top[:, :HD]
        total = jnp.zeros((1, BLOCK), f32)
        drop = jnp.zeros((1, BLOCK), f32)
        for kind in (0, 1):
            for t in range(i + 1):
                rows = slice(t * HD, (t + 1) * HD)
                e = jnp.exp2(e_own[i, kind, rows] - top)
                dp = dot_nt(v_all[kind][rows], gs[i])
                total = total + jnp.sum(e, 0, keepdims=True)
                drop = drop + jnp.sum(e * dp, 0, keepdims=True)
                e_own[i, kind, rows] = e
                dp_own[i, kind, rows] = dp
        totals.append(total)
        drops.append(drop)
    for i in range(blocks):
        at = pl.ds(i * HD, HD)
        stat[1, 0:1, at] = totals[i][:, :HD]
        stat[2, 0:1, at] = drops[i][:, :HD]

    @pl.when(half == 1)
    def _():
        v0 = tile_rows(recvx, 1)
        dk, dv = None, None
        for c in range(0, SEG_ROWS, BLOCK):
            at = pl.ds(c, BLOCK)
            query, grad = q_all[0][c : c + BLOCK], g_all[0][c : c + BLOCK]
            top = stat[0, 0:1, at]
            total, drop = stat[1, 0:1, at], stat[2, 0:1, at]
            for r in range(0, SEG_ROWS, BLOCK):
                rows = pl.ds(r, BLOCK)
                e = jnp.exp2(s0[rows, at] - top)
                dp = dot_nt(v0[r : r + BLOCK], grad)
                total = total + jnp.sum(e, 0, keepdims=True)
                drop = drop + jnp.sum(e * dp, 0, keepdims=True)
                s0[rows, at] = e
                dp0[rows, at] = dp
            stat[1, 0:1, at] = total
            stat[2, 0:1, at] = drop
            inverse = 1.0 / total
            drop = drop * inverse
            for r in range(0, SEG_ROWS, BLOCK):
                rows = pl.ds(r, BLOCK)
                w = s0[rows, at] * inverse
                ds = (w * (dp0[rows, at] - drop)).astype(bf16)
                w = w.astype(bf16)
                ot0[:, at] += dot_nn(vt[2, :, rows], w)
                dqt0[:, at] += dot_nn(kt[2, :, rows], ds)
                dk, dv = dot_nn(ds, query), dot_nn(w, grad)
                if c:
                    dk = dk + dkv[0, 2, rows]
                    dv = dv + dkv[1, 2, rows]
                dkv[0, 2, rows] = dk
                dkv[1, 2, rows] = dv
        resx[:, :ROWS] = (dkv[0, 2] * SCORE_SCALE).astype(bf16).reshape(GROUP, ROWS, HD)
        resx[:, ROWS:] = dkv[1, 2].astype(bf16).reshape(GROUP, ROWS, HD)
        send_crosses()

    started = False
    for i in reversed(range(blocks)):
        at = pl.ds(i * HD, HD)
        n = (i + 1) * HD
        total = jnp.concatenate([stat[1, 0:1, at], totals[i][:, HD:]], 1)
        drop = jnp.concatenate([stat[2, 0:1, at], drops[i][:, HD:]], 1)
        inverse = 1.0 / total
        drop = drop * inverse
        out_t = jnp.concatenate([ot0[:, at], jnp.zeros((HD, HD), f32)], 1)
        dq_t = jnp.concatenate([dqt0[:, at], jnp.zeros((HD, HD), f32)], 1)
        for kind in (0, 1):
            w = e_own[i, kind, :n] * inverse
            ds = (w * (dp_own[i, kind, :n] - drop)).astype(bf16)
            w = w.astype(bf16)
            out_t = out_t + dot_nn(vt[kind, :, :n], w)
            dq_t = dq_t + dot_nn(kt[kind, :, :n], ds)
            dk, dv = dot_nn(ds, qs[i]), dot_nn(w, gs[i])
            if started:
                dk = dk + dkv[0, kind, :n]
                dv = dv + dkv[1, kind, :n]
            dkv[0, kind, :n] = dk
            dkv[1, kind, :n] = dv
        started = True
        out = dot_nt(eye_block, out_t.astype(bf16)).astype(bf16)
        dq = dot_nt(eye_block, (dq_t * SCORE_SCALE).astype(bf16)).astype(bf16)
        owners = slice(8 * i, 8 * i + 8)
        for kind in (0, 1):
            tiles = (
                out[kind * HD : (kind + 1) * HD],
                dq[kind * HD : (kind + 1) * HD],
                (dkv[0, kind, at] * SCORE_SCALE).astype(bf16),
                dkv[1, kind, at].astype(bf16),
            )
            for t, tile in enumerate(tiles):
                slot = (2 * t + kind) * ROWS
                res[owners, slot : slot + ROWS] = tile.reshape(8, ROWS, HD)
        send_back(i)


def place_kernel(back, backx, o_ref, dq_ref, dk_ref, dv_ref):
    first = lax.axis_index("seq") < GROUP
    for h in range(H):
        shape = (TOKENS, 2 * ROWS)
        rank = iota(shape, 1)
        kind = (h + FINEST * (rank >> 4)) & (CLASSES - 1)
        spread = (iota(shape, 0) == CLASSES * (rank & (ROWS - 1)) + kind).astype(jnp.bfloat16)
        lanes = pl.ds(h * HD, HD)
        for i, ref in enumerate((o_ref, dq_ref, dk_ref, dv_ref)):
            rows = back[h, 2 * i * ROWS : (2 * i + 2) * ROWS]
            if i >= 2:
                extra = jnp.where(first, backx[h, (i - 2) * ROWS : (i - 1) * ROWS].astype(jnp.float32), 0.0)
                summed = (rows[:ROWS].astype(jnp.float32) + extra).astype(jnp.bfloat16)
                rows = jnp.concatenate([summed, rows[ROWS:]], 0)
            ref[:, lanes] = dot_nn(spread, rows).astype(jnp.bfloat16)


def per_device(queries, keys, values, cotangent, doc_ids):
    any_space = pl.BlockSpec(memory_space=pl.ANY)
    vmem = pl.BlockSpec(memory_space=pltpu.VMEM)
    bf16, f32 = jnp.bfloat16, jnp.float32
    dma = pltpu.SemaphoreType.DMA
    back, backx = pl.pallas_call(
        exchange_kernel,
        out_shape=(
            jax.ShapeDtypeStruct((H, 8 * ROWS, HD), bf16),
            jax.ShapeDtypeStruct((H, 2 * ROWS, HD), bf16),
        ),
        in_specs=[any_space] * 4 + [vmem],
        out_specs=(any_space, any_space),
        scratch_shapes=[
            pltpu.VMEM((4, TOKENS, H * HD), bf16),
            pltpu.VMEM((H, MESSAGE, HD), bf16),
            pltpu.VMEM((GROUP, MESSAGE, HD), bf16),
            pltpu.VMEM((GROUP, CROSS, HD), bf16),
            pltpu.VMEM((GROUP, 8 * ROWS, HD), bf16),
            pltpu.VMEM((GROUP, 2 * ROWS, HD), bf16),
            pltpu.VMEM((3, HD, SEG_ROWS), bf16),
            pltpu.VMEM((3, HD, SEG_ROWS), bf16),
            pltpu.VMEM((SEG_ROWS, SEG_ROWS), f32),
            pltpu.VMEM((SEG_ROWS, SEG_ROWS), f32),
            pltpu.VMEM((SEG_ROWS // HD, 2, SEG_ROWS, BLOCK), f32),
            pltpu.VMEM((SEG_ROWS // HD, 2, SEG_ROWS, BLOCK), f32),
            pltpu.VMEM((3, 8, SEG_ROWS), f32),
            pltpu.VMEM((HD, SEG_ROWS), f32),
            pltpu.VMEM((HD, SEG_ROWS), f32),
            pltpu.VMEM((2, 3, SEG_ROWS, HD), f32),
            dma((4,)),
            dma,
            dma,
            dma,
            dma,
            dma,
            dma,
        ],
        compiler_params=pltpu.CompilerParams(
            collective_id=0, has_side_effects=True, vmem_limit_bytes=62 * 2**20
        ),
        name="exchange",
    )(queries, keys, values, cotangent, doc_ids.reshape(1, TOKENS))
    full = jax.ShapeDtypeStruct((TOKENS, H * HD), bf16)
    return tuple(
        pl.pallas_call(
            place_kernel,
            out_shape=(full,) * 4,
            in_specs=[vmem, vmem],
            out_specs=(vmem,) * 4,
            name="place",
        )(back, backx)
    )


def solution(mesh):
    spec = P(("dp", "seq"), None)
    return jax.shard_map(
        per_device,
        mesh=mesh,
        in_specs=(spec, spec, spec, spec, P(("dp", "seq"))),
        out_specs=(spec,) * 4,
        check_vma=False,
    )
```

```python
import jax
import jax.numpy as jnp
from jax import lax
from jax.experimental import pallas as pl
from jax.experimental.pallas import tpu as pltpu
from jax.sharding import PartitionSpec as P

H = 8
HD = 128
SEQ_DEVICES = 64
GROUP = 32
TOKENS = 128
ROWS = 16
SEG_ROWS = GROUP * ROWS
BLOCK = 256
CLASSES = 8
FINEST = 4
SCORE_SCALE = HD**-0.5
LOG2_E = 1.4426950408889634
MASKED = -1e30
MESH_ID = pl.DeviceIdType.MESH

MESSAGE = 8 * ROWS + 8
CROSS_AT = 6 * ROWS
CROSS = MESSAGE - CROSS_AT

Q_OF, K_OF, V_OF, D_OF = (0, 1), (6, 4), (7, 5), (2, 3)


def dot_nn(a, b):
    return jnp.dot(a, b, preferred_element_type=jnp.float32)


def dot_nt(a, b):
    return lax.dot_general(a, b, (((1,), (1,)), ((), ())), preferred_element_type=jnp.float32)


def iota(shape, dim):
    return lax.broadcasted_iota(jnp.int32, shape, dim)


def selector(head):
    shape = (2 * ROWS, TOKENS)
    row = iota(shape, 0)
    kind = (head + FINEST * (row >> 4)) & (CLASSES - 1)
    return iota(shape, 1) == CLASSES * (row & (ROWS - 1)) + kind


def worker_of(head, half):
    return GROUP * half + 8 + 2 * head


def exchange_kernel(
    q_hbm, k_hbm, v_hbm, g_hbm, doc_hbm, back, backx,
    doc_ref, xin, snd, recv, recvx, res, resx, kt, vt, s0, dp0, e_own, dp_own, stat, ot0, dqt0, dkv,
    in_sem, send_sem, recv_sem, recvx_sem, ret_sem, back_sem, backx_sem,
):
    me = lax.axis_index("seq")
    half = me // GROUP
    rank = lax.rem(me, GROUP)
    is_worker = (rank >= 8) & (rank < 24) & (lax.rem(rank, 2) == 0)
    head = (rank - 8) // 2

    loads = [
        pltpu.make_async_copy(ref, xin.at[i], in_sem.at[i])
        for i, ref in enumerate((q_hbm, k_hbm, v_hbm, g_hbm))
    ]
    load_docs = pltpu.make_async_copy(doc_hbm, doc_ref, in_sem.at[4])
    load_docs.start()
    for load in loads:
        load.start()

    barrier = pltpu.get_barrier_semaphore()

    def greet(device):
        @pl.when(device != me)
        def _():
            pl.semaphore_signal(barrier, inc=1, device_id={"seq": device}, device_id_type=MESH_ID)

    @pl.when(is_worker)
    def _():
        lax.fori_loop(0, GROUP * (1 + half), lambda i, c: (greet(i), c)[1], 0)

    load_docs.wait()
    docs = jnp.broadcast_to(doc_ref[...].astype(jnp.float32), (8, TOKENS)).astype(jnp.bfloat16)
    for h in range(H):
        snd[h, 8 * ROWS : MESSAGE] = docs
    one_hots = [selector(h).astype(jnp.bfloat16) for h in range(H)]
    for i, slots in enumerate((Q_OF, K_OF, V_OF, D_OF)):
        loads[i].wait()
        for h in range(H):
            rows = dot_nn(one_hots[h], xin[i, :, h * HD : (h + 1) * HD]).astype(jnp.bfloat16)
            for kind, slot in enumerate(slots):
                snd[h, slot * ROWS : (slot + 1) * ROWS] = rows[kind * ROWS : (kind + 1) * ROWS]

    own_workers = jnp.where(half == 0, 2 * H, H) - jnp.where(is_worker, 1, 0)
    pl.semaphore_wait(barrier, own_workers)


    def send_main(h):
        return pltpu.make_async_remote_copy(
            snd.at[h], recv.at[rank], send_sem, recv_sem,
            device_id={"seq": worker_of(h, half)}, device_id_type=MESH_ID,
        )

    def send_cross(h):
        return pltpu.make_async_remote_copy(
            snd.at[h, pl.ds(CROSS_AT, CROSS)], recvx.at[rank], send_sem, recvx_sem,
            device_id={"seq": worker_of(h, 1)}, device_id_type=MESH_ID,
        )

    def wave_head(i):
        wave, k = i // 4, lax.rem(i + me, 4)
        return 2 * k + jnp.where(k < 2, wave, 1 - wave)

    def send_head(i, carry):
        h = wave_head(i)
        target = worker_of(h, half)

        @pl.when(target != me)
        def _():
            send_main(h).start()

        @pl.when(target == me)
        def _():
            pltpu.make_async_copy(snd.at[h], recv.at[rank], recv_sem).start()

        return carry

    def send_cross_head(i, carry):
        send_cross(wave_head(i)).start()
        return carry

    for wave in range(2):
        @pl.when(half == 0)
        def _():
            lax.fori_loop(4 * wave, 4 * wave + 4, send_cross_head, 0)

        lax.fori_loop(4 * wave, 4 * wave + 4, send_head, 0)

    @pl.when(is_worker)
    def _():
        pltpu.make_async_copy(recv, recv, recv_sem).wait()

        @pl.when(half == 1)
        def _():
            pltpu.make_async_copy(recvx, recvx, recvx_sem).wait()

        def send_cross_back(i, carry):
            r = lax.rem(i + rank, GROUP)
            pltpu.make_async_remote_copy(
                resx.at[r], backx.at[head], ret_sem, backx_sem,
                device_id={"seq": r}, device_id_type=MESH_ID,
            ).start()
            return carry

        def send_back(block):
            def one(i, carry):
                r = block * 8 + lax.rem(i + rank, 8)
                target = GROUP * half + r

                @pl.when(target != me)
                def _():
                    pltpu.make_async_remote_copy(
                        res.at[r], back.at[head], ret_sem, back_sem,
                        device_id={"seq": target}, device_id_type=MESH_ID,
                    ).start()

                @pl.when(target == me)
                def _():
                    pltpu.make_async_copy(res.at[r], back.at[head], back_sem).start()

                return carry

            lax.fori_loop(0, 8, one, 0)

        def send_crosses():
            lax.fori_loop(0, GROUP, send_cross_back, 0)

        attention(
            head, half, recv, recvx, res, resx, kt, vt, s0, dp0, e_own, dp_own, stat, ot0, dqt0, dkv,
            send_crosses, send_back,
        )

    pltpu.make_async_copy(back, back, back_sem).wait()

    @pl.when(half == 0)
    def _():
        pltpu.make_async_copy(backx, backx, backx_sem).wait()

    def sent_head(h, carry):
        @pl.when(worker_of(h, half) != me)
        def _():
            send_main(h).wait_send()

        @pl.when(half == 0)
        def _():
            send_cross(h).wait_send()

        return carry

    lax.fori_loop(0, H, sent_head, 0)

    @pl.when(is_worker)
    def _():
        def sent_back(i, carry):
            @pl.when(GROUP * half + i != me)
            def _():
                pltpu.make_async_remote_copy(
                    res.at[i], back.at[head], ret_sem, back_sem,
                    device_id={"seq": i}, device_id_type=MESH_ID,
                ).wait_send()

            @pl.when(half == 1)
            def _():
                pltpu.make_async_remote_copy(
                    resx.at[i], backx.at[head], ret_sem, backx_sem,
                    device_id={"seq": i}, device_id_type=MESH_ID,
                ).wait_send()

            return carry

        lax.fori_loop(0, GROUP, sent_back, 0)


def tile_rows(ref, tile):
    return ref[:, tile * ROWS : (tile + 1) * ROWS].reshape(SEG_ROWS, HD)


def class_docs(ref, at, kind):
    eight = ref[:, at : at + 8].astype(jnp.float32)
    spread = jnp.concatenate([eight, eight], 1).reshape(SEG_ROWS, HD)
    shape = (SEG_ROWS, HD)
    own = iota(shape, 1) == CLASSES * (iota(shape, 0) & (ROWS - 1)) + kind
    picked = jnp.where(own, spread, 0.0).astype(jnp.bfloat16)
    ones = jnp.ones((HD, HD), jnp.bfloat16)
    return dot_nn(picked, ones), dot_nt(ones[:8], picked)


def attention(
    head, half, recv, recvx, res, resx, kt, vt, s0, dp0, e_own, dp_own, stat, ot0, dqt0, dkv,
    send_crosses, send_back,
):
    bf16, f32 = jnp.bfloat16, jnp.float32
    scale = SCORE_SCALE * LOG2_E
    eye = (iota((HD, HD), 0) == iota((HD, HD), 1)).astype(bf16)
    eye_block = (iota((BLOCK, BLOCK), 0) == iota((BLOCK, BLOCK), 1)).astype(bf16)
    q_all = [tile_rows(recv, t) for t in Q_OF]
    k_all = [tile_rows(recv, t) for t in K_OF]
    v_all = [tile_rows(recv, t) for t in V_OF]
    g_all = [tile_rows(recv, t) for t in D_OF]
    for kind in (0, 1):
        kt[kind] = dot_nt(eye, k_all[kind]).astype(bf16)
        vt[kind] = dot_nt(eye, v_all[kind]).astype(bf16)
    docs = [class_docs(recv, 8 * ROWS, (head + FINEST * kind) & (CLASSES - 1)) for kind in (0, 1)]
    cols = [d[0] for d in docs]
    q_docs = [d[1][0:1] for d in docs]

    stat[0] = jnp.full((8, SEG_ROWS), MASKED, f32)
    stat[1] = jnp.zeros((8, SEG_ROWS), f32)
    stat[2] = jnp.zeros((8, SEG_ROWS), f32)
    ot0[...] = jnp.zeros_like(ot0)
    dqt0[...] = jnp.zeros_like(dqt0)

    @pl.when(half == 1)
    def _():
        col0, _ = class_docs(recvx, 2 * ROWS, head)
        k0 = tile_rows(recvx, 0)
        kt[2] = dot_nt(eye, k0).astype(bf16)
        vt[2] = dot_nt(eye, tile_rows(recvx, 1)).astype(bf16)
        for c in range(0, SEG_ROWS, BLOCK):
            at = pl.ds(c, BLOCK)
            query = q_all[0][c : c + BLOCK]
            top = None
            for r in range(0, SEG_ROWS, BLOCK):
                doc = col0[r : r + BLOCK]
                s = dot_nt(k0[r : r + BLOCK], query) * scale
                allowed = jnp.concatenate([doc, doc], 1) == q_docs[0][:, c : c + BLOCK]
                s = jnp.where(allowed, s, MASKED)
                s0[pl.ds(r, BLOCK), at] = s
                t = jnp.max(s, 0, keepdims=True)
                top = t if top is None else jnp.maximum(top, t)
            stat[0, 0:1, at] = top

    lower = iota((HD, BLOCK), 0) - (iota((HD, BLOCK), 1) & (HD - 1))
    is_a = iota((HD, BLOCK), 1) < HD
    b_is_later = jnp.where(head < FINEST, 1, 0)
    in_order = [
        lower <= jnp.where(is_a, 0, b_is_later - 1),
        lower <= jnp.where(is_a, -b_is_later, 0),
    ]
    bonus = jnp.where(iota((1, BLOCK), 1) < HD, 1.0, 0.0)
    both = lambda pair, i: jnp.concatenate([pair[0][i * HD : (i + 1) * HD], pair[1][i * HD : (i + 1) * HD]], 0)
    lanes = lambda pair, i: jnp.concatenate([pair[0][:, i * HD : (i + 1) * HD], pair[1][:, i * HD : (i + 1) * HD]], 1)
    blocks = SEG_ROWS // HD
    qs = [both(q_all, i) for i in range(blocks)]
    gs = [both(g_all, i) for i in range(blocks)]
    totals, drops = [], []
    for i in range(blocks):
        query_docs = lanes(q_docs, i)
        at = pl.ds(i * HD, HD)
        top = jnp.concatenate([stat[0, 0:1, at], jnp.full((1, HD), MASKED, f32)], 1)
        for kind in (0, 1):
            for t in range(i + 1):
                rows = slice(t * HD, (t + 1) * HD)
                s = dot_nt(k_all[kind][rows], qs[i]) * scale
                if kind == 0:
                    s = s + bonus
                doc = cols[kind][rows]
                allowed = jnp.concatenate([doc, doc], 1) == query_docs
                if t == i:
                    allowed = allowed & in_order[kind]
                s = jnp.where(allowed, s, MASKED)
                e_own[i, kind, rows] = s
                top = jnp.maximum(top, jnp.max(s, 0, keepdims=True))
        stat[0, 0:1, at] = top[:, :HD]
        total = jnp.zeros((1, BLOCK), f32)
        drop = jnp.zeros((1, BLOCK), f32)
        for kind in (0, 1):
            for t in range(i + 1):
                rows = slice(t * HD, (t + 1) * HD)
                e = jnp.exp2(e_own[i, kind, rows] - top)
                dp = dot_nt(v_all[kind][rows], gs[i])
                total = total + jnp.sum(e, 0, keepdims=True)
                drop = drop + jnp.sum(e * dp, 0, keepdims=True)
                e_own[i, kind, rows] = e
                dp_own[i, kind, rows] = dp
        totals.append(total)
        drops.append(drop)
    for i in range(blocks):
        at = pl.ds(i * HD, HD)
        stat[1, 0:1, at] = totals[i][:, :HD]
        stat[2, 0:1, at] = drops[i][:, :HD]

    @pl.when(half == 1)
    def _():
        v0 = tile_rows(recvx, 1)
        dk, dv = None, None
        for c in range(0, SEG_ROWS, BLOCK):
            at = pl.ds(c, BLOCK)
            query, grad = q_all[0][c : c + BLOCK], g_all[0][c : c + BLOCK]
            top = stat[0, 0:1, at]
            total, drop = stat[1, 0:1, at], stat[2, 0:1, at]
            for r in range(0, SEG_ROWS, BLOCK):
                rows = pl.ds(r, BLOCK)
                e = jnp.exp2(s0[rows, at] - top)
                dp = dot_nt(v0[r : r + BLOCK], grad)
                total = total + jnp.sum(e, 0, keepdims=True)
                drop = drop + jnp.sum(e * dp, 0, keepdims=True)
                s0[rows, at] = e
                dp0[rows, at] = dp
            stat[1, 0:1, at] = total
            stat[2, 0:1, at] = drop
            inverse = 1.0 / total
            drop = drop * inverse
            for r in range(0, SEG_ROWS, BLOCK):
                rows = pl.ds(r, BLOCK)
                w = s0[rows, at] * inverse
                ds = (w * (dp0[rows, at] - drop)).astype(bf16)
                w = w.astype(bf16)
                ot0[:, at] += dot_nn(vt[2, :, rows], w)
                dqt0[:, at] += dot_nn(kt[2, :, rows], ds)
                dk, dv = dot_nn(ds, query), dot_nn(w, grad)
                if c:
                    dk = dk + dkv[0, 2, rows]
                    dv = dv + dkv[1, 2, rows]
                dkv[0, 2, rows] = dk
                dkv[1, 2, rows] = dv
        resx[:, :ROWS] = (dkv[0, 2] * SCORE_SCALE).astype(bf16).reshape(GROUP, ROWS, HD)
        resx[:, ROWS:] = dkv[1, 2].astype(bf16).reshape(GROUP, ROWS, HD)
        send_crosses()

    started = False
    for i in reversed(range(blocks)):
        at = pl.ds(i * HD, HD)
        n = (i + 1) * HD
        total = jnp.concatenate([stat[1, 0:1, at], totals[i][:, HD:]], 1)
        drop = jnp.concatenate([stat[2, 0:1, at], drops[i][:, HD:]], 1)
        inverse = 1.0 / total
        drop = drop * inverse
        out_t = jnp.concatenate([ot0[:, at], jnp.zeros((HD, HD), f32)], 1)
        dq_t = jnp.concatenate([dqt0[:, at], jnp.zeros((HD, HD), f32)], 1)
        for kind in (0, 1):
            w = e_own[i, kind, :n] * inverse
            ds = (w * (dp_own[i, kind, :n] - drop)).astype(bf16)
            w = w.astype(bf16)
            out_t = out_t + dot_nn(vt[kind, :, :n], w)
            dq_t = dq_t + dot_nn(kt[kind, :, :n], ds)
            dk, dv = dot_nn(ds, qs[i]), dot_nn(w, gs[i])
            if started:
                dk = dk + dkv[0, kind, :n]
                dv = dv + dkv[1, kind, :n]
            dkv[0, kind, :n] = dk
            dkv[1, kind, :n] = dv
        started = True
        out = dot_nt(eye_block, out_t.astype(bf16)).astype(bf16)
        dq = dot_nt(eye_block, (dq_t * SCORE_SCALE).astype(bf16)).astype(bf16)
        owners = slice(8 * i, 8 * i + 8)
        for kind in (0, 1):
            tiles = (
                out[kind * HD : (kind + 1) * HD],
                dq[kind * HD : (kind + 1) * HD],
                (dkv[0, kind, at] * SCORE_SCALE).astype(bf16),
                dkv[1, kind, at].astype(bf16),
            )
            for t, tile in enumerate(tiles):
                slot = (2 * t + kind) * ROWS
                res[owners, slot : slot + ROWS] = tile.reshape(8, ROWS, HD)
        send_back(i)


def place_kernel(back, backx, o_hbm, dq_hbm, dk_hbm, dv_hbm, rows_out, sems):
    first = lax.axis_index("seq") < GROUP
    copies = []
    for i, ref in enumerate((o_hbm, dq_hbm, dk_hbm, dv_hbm)):
        for h in range(H):
            shape = (TOKENS, 2 * ROWS)
            rank = iota(shape, 1)
            kind = (h + FINEST * (rank >> 4)) & (CLASSES - 1)
            spread = (iota(shape, 0) == CLASSES * (rank & (ROWS - 1)) + kind).astype(jnp.bfloat16)
            rows = back[h, 2 * i * ROWS : (2 * i + 2) * ROWS]
            if i >= 2:
                extra = backx[h, (i - 2) * ROWS : (i - 1) * ROWS].astype(jnp.float32)
                summed = rows[:ROWS].astype(jnp.float32) + jnp.where(first, extra, 0.0)
                rows = jnp.concatenate([summed.astype(jnp.bfloat16), rows[ROWS:]], 0)
            rows_out[i, :, h * HD : (h + 1) * HD] = dot_nn(spread, rows).astype(jnp.bfloat16)
        copies.append(pltpu.make_async_copy(rows_out.at[i], ref, sems.at[i]))
        copies[-1].start()
    for copy in copies:
        copy.wait()


def per_device(queries, keys, values, cotangent, doc_ids):
    any_space = pl.BlockSpec(memory_space=pl.ANY)
    vmem = pl.BlockSpec(memory_space=pltpu.VMEM)
    bf16, f32 = jnp.bfloat16, jnp.float32
    dma = pltpu.SemaphoreType.DMA
    back, backx = pl.pallas_call(
        exchange_kernel,
        out_shape=(
            jax.ShapeDtypeStruct((H, 8 * ROWS, HD), bf16),
            jax.ShapeDtypeStruct((H, 2 * ROWS, HD), bf16),
        ),
        in_specs=[any_space] * 5,
        out_specs=(any_space, any_space),
        scratch_shapes=[
            pltpu.VMEM((1, TOKENS), jnp.int32),
            pltpu.VMEM((4, TOKENS, H * HD), bf16),
            pltpu.VMEM((H, MESSAGE, HD), bf16),
            pltpu.VMEM((GROUP, MESSAGE, HD), bf16),
            pltpu.VMEM((GROUP, CROSS, HD), bf16),
            pltpu.VMEM((GROUP, 8 * ROWS, HD), bf16),
            pltpu.VMEM((GROUP, 2 * ROWS, HD), bf16),
            pltpu.VMEM((3, HD, SEG_ROWS), bf16),
            pltpu.VMEM((3, HD, SEG_ROWS), bf16),
            pltpu.VMEM((SEG_ROWS, SEG_ROWS), f32),
            pltpu.VMEM((SEG_ROWS, SEG_ROWS), f32),
            pltpu.VMEM((SEG_ROWS // HD, 2, SEG_ROWS, BLOCK), f32),
            pltpu.VMEM((SEG_ROWS // HD, 2, SEG_ROWS, BLOCK), f32),
            pltpu.VMEM((3, 8, SEG_ROWS), f32),
            pltpu.VMEM((HD, SEG_ROWS), f32),
            pltpu.VMEM((HD, SEG_ROWS), f32),
            pltpu.VMEM((2, 3, SEG_ROWS, HD), f32),
            dma((5,)),
            dma,
            dma,
            dma,
            dma,
            dma,
            dma,
        ],
        compiler_params=pltpu.CompilerParams(
            collective_id=0, has_side_effects=True, vmem_limit_bytes=28 * 2**20
        ),
        name="exchange",
    )(*[pltpu.with_memory_space_constraint(a, pltpu.HBM) for a in (queries, keys, values, cotangent, doc_ids.reshape(1, TOKENS))])
    full = jax.ShapeDtypeStruct((TOKENS, H * HD), bf16)
    return tuple(
        pl.pallas_call(
            place_kernel,
            out_shape=(full,) * 4,
            in_specs=[vmem, vmem],
            out_specs=(any_space,) * 4,
            scratch_shapes=[pltpu.VMEM((4, TOKENS, H * HD), bf16), dma((4,))],
            compiler_params=pltpu.CompilerParams(vmem_limit_bytes=16 * 2**20),
            name="place",
        )(back, backx)
    )


def solution(mesh):
    spec = P(("dp", "seq"), None)
    return jax.shard_map(
        per_device,
        mesh=mesh,
        in_specs=(spec, spec, spec, spec, P(("dp", "seq"))),
        out_specs=(spec,) * 4,
        check_vma=False,
    )
```

```python
import jax
import jax.numpy as jnp
from jax import lax
from jax.experimental import pallas as pl
from jax.experimental.pallas import tpu as pltpu
from jax.sharding import PartitionSpec as P

H = 8
HD = 128
SEQ_DEVICES = 64
GROUP = 32
TOKENS = 128
ROWS = 16
SEG_ROWS = GROUP * ROWS
BLOCK = 256
CLASSES = 8
FINEST = 4
SCORE_SCALE = HD**-0.5
LOG2_E = 1.4426950408889634
MASKED = -1e30
MESH_ID = pl.DeviceIdType.MESH

MESSAGE = 8 * ROWS
CROSS_AT = 6 * ROWS
CROSS = MESSAGE - CROSS_AT

Q_OF, K_OF, V_OF, D_OF = (0, 1), (6, 4), (7, 5), (2, 3)


def dot_nn(a, b):
    return jnp.dot(a, b, preferred_element_type=jnp.float32)


def dot_nt(a, b):
    return lax.dot_general(a, b, (((1,), (1,)), ((), ())), preferred_element_type=jnp.float32)


def iota(shape, dim):
    return lax.broadcasted_iota(jnp.int32, shape, dim)


def selector(head):
    shape = (2 * ROWS, TOKENS)
    row = iota(shape, 0)
    kind = (head + FINEST * (row >> 4)) & (CLASSES - 1)
    return iota(shape, 1) == CLASSES * (row & (ROWS - 1)) + kind


def worker_of(head, half):
    return GROUP * half + 8 + 2 * head


def exchange_kernel(
    q_hbm, k_hbm, v_hbm, g_hbm, doc_hbm, back, backx,
    doc_ref, docs_in, xin, snd, recv, recvx, res, resx, kt, vt, s0, dp0, e_own, dp_own, stat, ot0, dqt0, dkv,
    in_sem, send_sem, recv_sem, recvx_sem, ret_sem, back_sem, backx_sem, docs_sem,
):
    me = lax.axis_index("seq")
    half = me // GROUP
    rank = lax.rem(me, GROUP)
    is_worker = (rank >= 8) & (rank < 24) & (lax.rem(rank, 2) == 0)
    head = (rank - 8) // 2

    loads = [
        pltpu.make_async_copy(ref, xin.at[i], in_sem.at[i])
        for i, ref in enumerate((q_hbm, k_hbm, v_hbm, g_hbm))
    ]
    load_docs = pltpu.make_async_copy(doc_hbm, doc_ref, in_sem.at[4])
    load_docs.start()
    for load in loads:
        load.start()

    barrier = pltpu.get_barrier_semaphore()

    def greet(device):
        @pl.when(device != me)
        def _():
            pl.semaphore_signal(barrier, inc=1, device_id={"seq": device}, device_id_type=MESH_ID)

    @pl.when(is_worker)
    def _():
        lax.fori_loop(0, GROUP * (1 + half), lambda i, c: (greet(i), c)[1], 0)

    load_docs.wait()
    one_hots = [selector(h).astype(jnp.bfloat16) for h in range(H)]
    for i, slots in enumerate((Q_OF, K_OF, V_OF, D_OF)):
        loads[i].wait()
        for h in range(H):
            rows = dot_nn(one_hots[h], xin[i, :, h * HD : (h + 1) * HD]).astype(jnp.bfloat16)
            for kind, slot in enumerate(slots):
                snd[h, slot * ROWS : (slot + 1) * ROWS] = rows[kind * ROWS : (kind + 1) * ROWS]

    own_workers = jnp.where(half == 0, 2 * H, H) - jnp.where(is_worker, 1, 0)
    pl.semaphore_wait(barrier, own_workers)


    def send_main(h):
        return pltpu.make_async_remote_copy(
            snd.at[h], recv.at[rank], send_sem, recv_sem,
            device_id={"seq": worker_of(h, half)}, device_id_type=MESH_ID,
        )

    def send_docs(h, to):
        return pltpu.make_async_remote_copy(
            doc_ref, docs_in.at[me], send_sem, docs_sem,
            device_id={"seq": worker_of(h, to)}, device_id_type=MESH_ID,
        )

    def send_cross(h):
        return pltpu.make_async_remote_copy(
            snd.at[h, pl.ds(CROSS_AT, CROSS)], recvx.at[rank], send_sem, recvx_sem,
            device_id={"seq": worker_of(h, 1)}, device_id_type=MESH_ID,
        )

    def wave_head(i):
        wave, k = i // 4, lax.rem(i + me, 4)
        return 2 * k + jnp.where(k < 2, wave, 1 - wave)

    def send_head(i, carry):
        h = wave_head(i)
        target = worker_of(h, half)

        @pl.when(target != me)
        def _():
            send_docs(h, half).start()
            send_main(h).start()

        @pl.when(target == me)
        def _():
            pltpu.make_async_copy(doc_ref, docs_in.at[me], docs_sem).start()
            pltpu.make_async_copy(snd.at[h], recv.at[rank], recv_sem).start()

        return carry

    def send_cross_head(i, carry):
        send_docs(wave_head(i), 1).start()
        send_cross(wave_head(i)).start()
        return carry

    for wave in range(2):
        @pl.when(half == 0)
        def _():
            lax.fori_loop(4 * wave, 4 * wave + 4, send_cross_head, 0)

        lax.fori_loop(4 * wave, 4 * wave + 4, send_head, 0)

    @pl.when(is_worker)
    def _():
        pltpu.make_async_copy(recv, recv, recv_sem).wait()

        @pl.when(half == 0)
        def _():
            first = docs_in.at[pl.ds(0, GROUP)]
            pltpu.make_async_copy(first, first, docs_sem).wait()

        @pl.when(half == 1)
        def _():
            pltpu.make_async_copy(docs_in, docs_in, docs_sem).wait()
            pltpu.make_async_copy(recvx, recvx, recvx_sem).wait()

        def send_cross_back(i, carry):
            j = i // 2
            r = 8 * (j // 8) + lax.rem(j + rank // 2, 8)
            r = jnp.where(lax.rem(i, 2) == 0, r, GROUP - 1 - r)
            pltpu.make_async_remote_copy(
                resx.at[r], backx.at[head], ret_sem, backx_sem,
                device_id={"seq": r}, device_id_type=MESH_ID,
            ).start()
            return carry

        def send_back(block):
            def one(i, carry):
                r = block * 8 + lax.rem(i + rank, 8)
                target = GROUP * half + r

                @pl.when(target != me)
                def _():
                    pltpu.make_async_remote_copy(
                        res.at[r], back.at[head], ret_sem, back_sem,
                        device_id={"seq": target}, device_id_type=MESH_ID,
                    ).start()

                @pl.when(target == me)
                def _():
                    pltpu.make_async_copy(res.at[r], back.at[head], back_sem).start()

                return carry

            lax.fori_loop(0, 8, one, 0)

        def send_crosses():
            lax.fori_loop(0, GROUP, send_cross_back, 0)

        attention(
            head, half, recv, recvx, docs_in, res, resx, kt, vt, s0, dp0, e_own, dp_own, stat, ot0, dqt0, dkv,
            send_crosses, send_back,
        )

    pltpu.make_async_copy(back, back, back_sem).wait()

    @pl.when(half == 0)
    def _():
        pltpu.make_async_copy(backx, backx, backx_sem).wait()

    def sent_head(h, carry):
        @pl.when(worker_of(h, half) != me)
        def _():
            send_docs(h, half).wait_send()
            send_main(h).wait_send()

        @pl.when(half == 0)
        def _():
            send_docs(h, 1).wait_send()
            send_cross(h).wait_send()

        return carry

    lax.fori_loop(0, H, sent_head, 0)

    @pl.when(is_worker)
    def _():
        def sent_back(i, carry):
            @pl.when(GROUP * half + i != me)
            def _():
                pltpu.make_async_remote_copy(
                    res.at[i], back.at[head], ret_sem, back_sem,
                    device_id={"seq": i}, device_id_type=MESH_ID,
                ).wait_send()

            @pl.when(half == 1)
            def _():
                pltpu.make_async_remote_copy(
                    resx.at[i], backx.at[head], ret_sem, backx_sem,
                    device_id={"seq": i}, device_id_type=MESH_ID,
                ).wait_send()

            return carry

        lax.fori_loop(0, GROUP, sent_back, 0)


def tile_rows(ref, tile):
    return ref[:, tile * ROWS : (tile + 1) * ROWS].reshape(SEG_ROWS, HD)


def class_docs(ref, at, kind):
    own_docs = ref[pl.ds(at, GROUP)].astype(jnp.float32)
    spread = jnp.broadcast_to(own_docs, (GROUP, ROWS, HD)).reshape(SEG_ROWS, HD)
    shape = (SEG_ROWS, HD)
    own = iota(shape, 1) == CLASSES * (iota(shape, 0) & (ROWS - 1)) + kind
    picked = jnp.where(own, spread, 0.0).astype(jnp.bfloat16)
    ones = jnp.ones((HD, HD), jnp.bfloat16)
    return dot_nn(picked, ones), dot_nt(ones[:8], picked)


def attention(
    head, half, recv, recvx, docs_in, res, resx, kt, vt, s0, dp0, e_own, dp_own, stat, ot0, dqt0, dkv,
    send_crosses, send_back,
):
    bf16, f32 = jnp.bfloat16, jnp.float32
    scale = SCORE_SCALE * LOG2_E
    eye = (iota((HD, HD), 0) == iota((HD, HD), 1)).astype(bf16)
    eye_block = (iota((BLOCK, BLOCK), 0) == iota((BLOCK, BLOCK), 1)).astype(bf16)
    q_all = [tile_rows(recv, t) for t in Q_OF]
    k_all = [tile_rows(recv, t) for t in K_OF]
    v_all = [tile_rows(recv, t) for t in V_OF]
    g_all = [tile_rows(recv, t) for t in D_OF]
    for kind in (0, 1):
        kt[kind] = dot_nt(eye, k_all[kind]).astype(bf16)
        vt[kind] = dot_nt(eye, v_all[kind]).astype(bf16)
    docs = [class_docs(docs_in, GROUP * half, (head + FINEST * kind) & (CLASSES - 1)) for kind in (0, 1)]
    cols = [d[0] for d in docs]
    q_docs = [d[1][0:1] for d in docs]

    stat[0] = jnp.full((8, SEG_ROWS), MASKED, f32)
    stat[1] = jnp.zeros((8, SEG_ROWS), f32)
    stat[2] = jnp.zeros((8, SEG_ROWS), f32)
    ot0[...] = jnp.zeros_like(ot0)
    dqt0[...] = jnp.zeros_like(dqt0)

    @pl.when(half == 1)
    def _():
        col0, _ = class_docs(docs_in, 0, head)
        k0 = tile_rows(recvx, 0)
        kt[2] = dot_nt(eye, k0).astype(bf16)
        vt[2] = dot_nt(eye, tile_rows(recvx, 1)).astype(bf16)
        for c in range(0, SEG_ROWS, BLOCK):
            at = pl.ds(c, BLOCK)
            query = q_all[0][c : c + BLOCK]
            top = None
            for r in range(0, SEG_ROWS, BLOCK):
                doc = col0[r : r + BLOCK]
                s = dot_nt(k0[r : r + BLOCK], query) * scale
                allowed = jnp.concatenate([doc, doc], 1) == q_docs[0][:, c : c + BLOCK]
                s = jnp.where(allowed, s, MASKED)
                s0[pl.ds(r, BLOCK), at] = s
                t = jnp.max(s, 0, keepdims=True)
                top = t if top is None else jnp.maximum(top, t)
            stat[0, 0:1, at] = top

    lower = iota((HD, BLOCK), 0) - (iota((HD, BLOCK), 1) & (HD - 1))
    is_a = iota((HD, BLOCK), 1) < HD
    b_is_later = jnp.where(head < FINEST, 1, 0)
    in_order = [
        lower <= jnp.where(is_a, 0, b_is_later - 1),
        lower <= jnp.where(is_a, -b_is_later, 0),
    ]
    bonus = jnp.where(iota((1, BLOCK), 1) < HD, 1.0, 0.0)
    both = lambda pair, i: jnp.concatenate([pair[0][i * HD : (i + 1) * HD], pair[1][i * HD : (i + 1) * HD]], 0)
    lanes = lambda pair, i: jnp.concatenate([pair[0][:, i * HD : (i + 1) * HD], pair[1][:, i * HD : (i + 1) * HD]], 1)
    blocks = SEG_ROWS // HD
    qs = [both(q_all, i) for i in range(blocks)]
    gs = [both(g_all, i) for i in range(blocks)]
    totals, drops = [], []
    for i in range(blocks):
        query_docs = lanes(q_docs, i)
        at = pl.ds(i * HD, HD)
        top = jnp.concatenate([stat[0, 0:1, at], jnp.full((1, HD), MASKED, f32)], 1)
        for kind in (0, 1):
            for t in range(i + 1):
                rows = slice(t * HD, (t + 1) * HD)
                s = dot_nt(k_all[kind][rows], qs[i]) * scale
                if kind == 0:
                    s = s + bonus
                doc = cols[kind][rows]
                allowed = jnp.concatenate([doc, doc], 1) == query_docs
                if t == i:
                    allowed = allowed & in_order[kind]
                s = jnp.where(allowed, s, MASKED)
                e_own[i, kind, rows] = s
                top = jnp.maximum(top, jnp.max(s, 0, keepdims=True))
        stat[0, 0:1, at] = top[:, :HD]
        total = jnp.zeros((1, BLOCK), f32)
        drop = jnp.zeros((1, BLOCK), f32)
        for kind in (0, 1):
            for t in range(i + 1):
                rows = slice(t * HD, (t + 1) * HD)
                e = jnp.exp2(e_own[i, kind, rows] - top)
                dp = dot_nt(v_all[kind][rows], gs[i])
                total = total + jnp.sum(e, 0, keepdims=True)
                drop = drop + jnp.sum(e * dp, 0, keepdims=True)
                e_own[i, kind, rows] = e
                dp_own[i, kind, rows] = dp
        totals.append(total)
        drops.append(drop)
    for i in range(blocks):
        at = pl.ds(i * HD, HD)
        stat[1, 0:1, at] = totals[i][:, :HD]
        stat[2, 0:1, at] = drops[i][:, :HD]

    @pl.when(half == 1)
    def _():
        v0 = tile_rows(recvx, 1)
        dk, dv = None, None
        for c in range(0, SEG_ROWS, BLOCK):
            at = pl.ds(c, BLOCK)
            query, grad = q_all[0][c : c + BLOCK], g_all[0][c : c + BLOCK]
            top = stat[0, 0:1, at]
            total, drop = stat[1, 0:1, at], stat[2, 0:1, at]
            for r in range(0, SEG_ROWS, BLOCK):
                rows = pl.ds(r, BLOCK)
                e = jnp.exp2(s0[rows, at] - top)
                dp = dot_nt(v0[r : r + BLOCK], grad)
                total = total + jnp.sum(e, 0, keepdims=True)
                drop = drop + jnp.sum(e * dp, 0, keepdims=True)
                s0[rows, at] = e
                dp0[rows, at] = dp
            stat[1, 0:1, at] = total
            stat[2, 0:1, at] = drop
            inverse = 1.0 / total
            drop = drop * inverse
            for r in range(0, SEG_ROWS, BLOCK):
                rows = pl.ds(r, BLOCK)
                w = s0[rows, at] * inverse
                ds = (w * (dp0[rows, at] - drop)).astype(bf16)
                w = w.astype(bf16)
                ot0[:, at] += dot_nn(vt[2, :, rows], w)
                dqt0[:, at] += dot_nn(kt[2, :, rows], ds)
                dk, dv = dot_nn(ds, query), dot_nn(w, grad)
                if c:
                    dk = dk + dkv[0, 2, rows]
                    dv = dv + dkv[1, 2, rows]
                dkv[0, 2, rows] = dk
                dkv[1, 2, rows] = dv
        resx[:, :ROWS] = (dkv[0, 2] * SCORE_SCALE).astype(bf16).reshape(GROUP, ROWS, HD)
        resx[:, ROWS:] = dkv[1, 2].astype(bf16).reshape(GROUP, ROWS, HD)
        send_crosses()

    started = False
    for i in reversed(range(blocks)):
        at = pl.ds(i * HD, HD)
        n = (i + 1) * HD
        total = jnp.concatenate([stat[1, 0:1, at], totals[i][:, HD:]], 1)
        drop = jnp.concatenate([stat[2, 0:1, at], drops[i][:, HD:]], 1)
        inverse = 1.0 / total
        drop = drop * inverse
        out_t = jnp.concatenate([ot0[:, at], jnp.zeros((HD, HD), f32)], 1)
        dq_t = jnp.concatenate([dqt0[:, at], jnp.zeros((HD, HD), f32)], 1)
        for kind in (0, 1):
            w = e_own[i, kind, :n] * inverse
            ds = (w * (dp_own[i, kind, :n] - drop)).astype(bf16)
            w = w.astype(bf16)
            out_t = out_t + dot_nn(vt[kind, :, :n], w)
            dq_t = dq_t + dot_nn(kt[kind, :, :n], ds)
            dk, dv = dot_nn(ds, qs[i]), dot_nn(w, gs[i])
            if started:
                dk = dk + dkv[0, kind, :n]
                dv = dv + dkv[1, kind, :n]
            dkv[0, kind, :n] = dk
            dkv[1, kind, :n] = dv
        started = True
        out = dot_nt(eye_block, out_t.astype(bf16)).astype(bf16)
        dq = dot_nt(eye_block, (dq_t * SCORE_SCALE).astype(bf16)).astype(bf16)
        owners = slice(8 * i, 8 * i + 8)
        for kind in (0, 1):
            tiles = (
                out[kind * HD : (kind + 1) * HD],
                dq[kind * HD : (kind + 1) * HD],
                (dkv[0, kind, at] * SCORE_SCALE).astype(bf16),
                dkv[1, kind, at].astype(bf16),
            )
            for t, tile in enumerate(tiles):
                slot = (2 * t + kind) * ROWS
                res[owners, slot : slot + ROWS] = tile.reshape(8, ROWS, HD)
        send_back(i)


def place_kernel(back, backx, o_hbm, dq_hbm, dk_hbm, dv_hbm, rows_out, sems):
    first = lax.axis_index("seq") < GROUP
    copies = []
    for i, ref in enumerate((o_hbm, dq_hbm, dk_hbm, dv_hbm)):
        for h in range(H):
            shape = (TOKENS, 2 * ROWS)
            rank = iota(shape, 1)
            kind = (h + FINEST * (rank >> 4)) & (CLASSES - 1)
            spread = (iota(shape, 0) == CLASSES * (rank & (ROWS - 1)) + kind).astype(jnp.bfloat16)
            rows = back[h, 2 * i * ROWS : (2 * i + 2) * ROWS]
            if i >= 2:
                extra = backx[h, (i - 2) * ROWS : (i - 1) * ROWS].astype(jnp.float32)
                summed = rows[:ROWS].astype(jnp.float32) + jnp.where(first, extra, 0.0)
                rows = jnp.concatenate([summed.astype(jnp.bfloat16), rows[ROWS:]], 0)
            rows_out[i, :, h * HD : (h + 1) * HD] = dot_nn(spread, rows).astype(jnp.bfloat16)
        copies.append(pltpu.make_async_copy(rows_out.at[i], ref, sems.at[i]))
        copies[-1].start()
    for copy in copies:
        copy.wait()


def per_device(queries, keys, values, cotangent, doc_ids):
    any_space = pl.BlockSpec(memory_space=pl.ANY)
    vmem = pl.BlockSpec(memory_space=pltpu.VMEM)
    bf16, f32 = jnp.bfloat16, jnp.float32
    dma = pltpu.SemaphoreType.DMA
    back, backx = pl.pallas_call(
        exchange_kernel,
        out_shape=(
            jax.ShapeDtypeStruct((H, 8 * ROWS, HD), bf16),
            jax.ShapeDtypeStruct((H, 2 * ROWS, HD), bf16),
        ),
        in_specs=[any_space] * 5,
        out_specs=(any_space, any_space),
        scratch_shapes=[
            pltpu.VMEM((1, TOKENS), jnp.int32),
            pltpu.VMEM((SEQ_DEVICES, 1, TOKENS), jnp.int32),
            pltpu.VMEM((4, TOKENS, H * HD), bf16),
            pltpu.VMEM((H, MESSAGE, HD), bf16),
            pltpu.VMEM((GROUP, MESSAGE, HD), bf16),
            pltpu.VMEM((GROUP, CROSS, HD), bf16),
            pltpu.VMEM((GROUP, 8 * ROWS, HD), bf16),
            pltpu.VMEM((GROUP, 2 * ROWS, HD), bf16),
            pltpu.VMEM((3, HD, SEG_ROWS), bf16),
            pltpu.VMEM((3, HD, SEG_ROWS), bf16),
            pltpu.VMEM((SEG_ROWS, SEG_ROWS), f32),
            pltpu.VMEM((SEG_ROWS, SEG_ROWS), f32),
            pltpu.VMEM((SEG_ROWS // HD, 2, SEG_ROWS, BLOCK), f32),
            pltpu.VMEM((SEG_ROWS // HD, 2, SEG_ROWS, BLOCK), f32),
            pltpu.VMEM((3, 8, SEG_ROWS), f32),
            pltpu.VMEM((HD, SEG_ROWS), f32),
            pltpu.VMEM((HD, SEG_ROWS), f32),
            pltpu.VMEM((2, 3, SEG_ROWS, HD), f32),
            dma((5,)),
            dma,
            dma,
            dma,
            dma,
            dma,
            dma,
            dma,
        ],
        compiler_params=pltpu.CompilerParams(
            collective_id=0, has_side_effects=True, vmem_limit_bytes=28 * 2**20
        ),
        name="exchange",
    )(*[pltpu.with_memory_space_constraint(a, pltpu.HBM) for a in (queries, keys, values, cotangent, doc_ids.reshape(1, TOKENS))])
    full = jax.ShapeDtypeStruct((TOKENS, H * HD), bf16)
    return tuple(
        pl.pallas_call(
            place_kernel,
            out_shape=(full,) * 4,
            in_specs=[vmem, vmem],
            out_specs=(any_space,) * 4,
            scratch_shapes=[pltpu.VMEM((4, TOKENS, H * HD), bf16), dma((4,))],
            compiler_params=pltpu.CompilerParams(vmem_limit_bytes=16 * 2**20),
            name="place",
        )(back, backx)
    )


def solution(mesh):
    spec = P(("dp", "seq"), None)
    return jax.shard_map(
        per_device,
        mesh=mesh,
        in_specs=(spec, spec, spec, spec, P(("dp", "seq"))),
        out_specs=(spec,) * 4,
        check_vma=False,
    )
```

```python
import jax
import jax.numpy as jnp
from jax import lax
from jax.experimental import pallas as pl
from jax.experimental.pallas import tpu as pltpu
from jax.sharding import PartitionSpec as P

H = 8
HD = 128
SEQ_DEVICES = 64
GROUP = 32
TOKENS = 128
ROWS = 16
SEG_ROWS = GROUP * ROWS
BLOCK = 256
CLASSES = 8
FINEST = 4
SCORE_SCALE = HD**-0.5
LOG2_E = 1.4426950408889634
MASKED = -1e30
MESH_ID = pl.DeviceIdType.MESH

MESSAGE = 8 * ROWS
CROSS_AT = 6 * ROWS
CROSS = MESSAGE - CROSS_AT

Q_OF, K_OF, V_OF, D_OF = (0, 1), (6, 4), (7, 5), (2, 3)


def dot_nn(a, b):
    return jnp.dot(a, b, preferred_element_type=jnp.float32)


def dot_nt(a, b):
    return lax.dot_general(a, b, (((1,), (1,)), ((), ())), preferred_element_type=jnp.float32)


def iota(shape, dim):
    return lax.broadcasted_iota(jnp.int32, shape, dim)


def selector(head):
    shape = (2 * ROWS, TOKENS)
    row = iota(shape, 0)
    kind = (head + FINEST * (row >> 4)) & (CLASSES - 1)
    return iota(shape, 1) == CLASSES * (row & (ROWS - 1)) + kind


def worker_of(head, half):
    return GROUP * half + 8 + 2 * head


def exchange_kernel(
    q_hbm, k_hbm, v_hbm, g_hbm, doc_hbm, back, backx,
    doc_ref, docs_in, xin, snd, recv, recvx, res, resx, kt, vt, s0, dp0, e_own, dp_own, stat, ot0, dqt0, dkv,
    in_sem, send_sem, recv_sem, recvx_sem, ret_sem, back_sem, backx_sem, docs_sem,
):
    me = lax.axis_index("seq")
    half = me // GROUP
    rank = lax.rem(me, GROUP)
    is_worker = (rank >= 8) & (rank < 24) & (lax.rem(rank, 2) == 0)
    head = (rank - 8) // 2

    loads = [
        pltpu.make_async_copy(ref, xin.at[i], in_sem.at[i])
        for i, ref in enumerate((q_hbm, k_hbm, v_hbm, g_hbm))
    ]
    load_docs = pltpu.make_async_copy(doc_hbm, doc_ref, in_sem.at[4])
    load_docs.start()
    for load in loads:
        load.start()

    barrier = pltpu.get_barrier_semaphore()

    def greet(device):
        @pl.when(device != me)
        def _():
            pl.semaphore_signal(barrier, inc=1, device_id={"seq": device}, device_id_type=MESH_ID)

    @pl.when(is_worker)
    def _():
        lax.fori_loop(0, GROUP * (1 + half), lambda i, c: (greet(i), c)[1], 0)

    load_docs.wait()
    one_hots = [selector(h).astype(jnp.bfloat16) for h in range(H)]
    for i, slots in enumerate((Q_OF, K_OF, V_OF, D_OF)):
        loads[i].wait()
        for h in range(H):
            rows = dot_nn(one_hots[h], xin[i, :, h * HD : (h + 1) * HD]).astype(jnp.bfloat16)
            for kind, slot in enumerate(slots):
                snd[h, slot * ROWS : (slot + 1) * ROWS] = rows[kind * ROWS : (kind + 1) * ROWS]

    own_workers = jnp.where(half == 0, 2 * H, H) - jnp.where(is_worker, 1, 0)
    pl.semaphore_wait(barrier, own_workers)


    def send_main(h):
        return pltpu.make_async_remote_copy(
            snd.at[h], recv.at[rank], send_sem, recv_sem,
            device_id={"seq": worker_of(h, half)}, device_id_type=MESH_ID,
        )

    def send_docs(h, to):
        return pltpu.make_async_remote_copy(
            doc_ref, docs_in.at[me], send_sem, docs_sem,
            device_id={"seq": worker_of(h, to)}, device_id_type=MESH_ID,
        )

    def send_cross(h):
        return pltpu.make_async_remote_copy(
            snd.at[h, pl.ds(CROSS_AT, CROSS)], recvx.at[rank], send_sem, recvx_sem,
            device_id={"seq": worker_of(h, 1)}, device_id_type=MESH_ID,
        )

    def wave_head(i):
        wave, k = i // 4, lax.rem(i + me, 4)
        return 2 * k + jnp.where(k < 2, wave, 1 - wave)

    def send_head(i, carry):
        h = wave_head(i)
        target = worker_of(h, half)

        @pl.when(target != me)
        def _():
            send_docs(h, half).start()
            send_main(h).start()

        @pl.when(target == me)
        def _():
            pltpu.make_async_copy(doc_ref, docs_in.at[me], docs_sem).start()
            pltpu.make_async_copy(snd.at[h], recv.at[rank], recv_sem).start()

        return carry

    def send_cross_head(i, carry):
        send_docs(wave_head(i), 1).start()
        send_cross(wave_head(i)).start()
        return carry

    for wave in range(2):
        @pl.when(half == 0)
        def _():
            lax.fori_loop(4 * wave, 4 * wave + 4, send_cross_head, 0)

        lax.fori_loop(4 * wave, 4 * wave + 4, send_head, 0)

    @pl.when(is_worker)
    def _():
        pltpu.make_async_copy(recv, recv, recv_sem).wait()

        @pl.when(half == 0)
        def _():
            first = docs_in.at[pl.ds(0, GROUP)]
            pltpu.make_async_copy(first, first, docs_sem).wait()

        @pl.when(half == 1)
        def _():
            pltpu.make_async_copy(docs_in, docs_in, docs_sem).wait()
            pltpu.make_async_copy(recvx, recvx, recvx_sem).wait()

        def send_cross_back(i, carry):
            j = i // 2
            r = 8 * (j // 8) + lax.rem(j + rank // 2, 8)
            r = jnp.where(lax.rem(i, 2) == 0, r, GROUP - 1 - r)
            pltpu.make_async_remote_copy(
                resx.at[r], backx.at[head], ret_sem, backx_sem,
                device_id={"seq": r}, device_id_type=MESH_ID,
            ).start()
            return carry

        def send_back(block, start, size):
            part = pl.ds(start, size)

            def one(i, carry):
                r = block * 8 + lax.rem(i + rank, 8)
                target = GROUP * half + r

                @pl.when(target != me)
                def _():
                    pltpu.make_async_remote_copy(
                        res.at[r, part], back.at[head, part], ret_sem, back_sem,
                        device_id={"seq": target}, device_id_type=MESH_ID,
                    ).start()

                @pl.when(target == me)
                def _():
                    pltpu.make_async_copy(res.at[r, part], back.at[head, part], back_sem).start()

                return carry

            lax.fori_loop(0, 8, one, 0)

        def send_crosses():
            lax.fori_loop(0, GROUP, send_cross_back, 0)

        attention(
            head, half, recv, recvx, docs_in, res, resx, kt, vt, s0, dp0, e_own, dp_own, stat, ot0, dqt0, dkv,
            send_crosses, send_back,
        )

    pltpu.make_async_copy(back, back, back_sem).wait()

    @pl.when(half == 0)
    def _():
        pltpu.make_async_copy(backx, backx, backx_sem).wait()

    def sent_head(h, carry):
        @pl.when(worker_of(h, half) != me)
        def _():
            send_docs(h, half).wait_send()
            send_main(h).wait_send()

        @pl.when(half == 0)
        def _():
            send_docs(h, 1).wait_send()
            send_cross(h).wait_send()

        return carry

    lax.fori_loop(0, H, sent_head, 0)

    @pl.when(is_worker)
    def _():
        def sent_back(i, carry):
            @pl.when(GROUP * half + i != me)
            def _():
                pltpu.make_async_remote_copy(
                    res.at[i], back.at[head], ret_sem, back_sem,
                    device_id={"seq": i}, device_id_type=MESH_ID,
                ).wait_send()

            @pl.when(half == 1)
            def _():
                pltpu.make_async_remote_copy(
                    resx.at[i], backx.at[head], ret_sem, backx_sem,
                    device_id={"seq": i}, device_id_type=MESH_ID,
                ).wait_send()

            return carry

        lax.fori_loop(0, GROUP, sent_back, 0)


def tile_rows(ref, tile):
    return ref[:, tile * ROWS : (tile + 1) * ROWS].reshape(SEG_ROWS, HD)


def class_docs(ref, at, kind):
    own_docs = ref[pl.ds(at, GROUP)].astype(jnp.float32)
    spread = jnp.broadcast_to(own_docs, (GROUP, ROWS, HD)).reshape(SEG_ROWS, HD)
    shape = (SEG_ROWS, HD)
    own = iota(shape, 1) == CLASSES * (iota(shape, 0) & (ROWS - 1)) + kind
    picked = jnp.where(own, spread, 0.0).astype(jnp.bfloat16)
    ones = jnp.ones((HD, HD), jnp.bfloat16)
    return dot_nn(picked, ones), dot_nt(ones[:8], picked)


def attention(
    head, half, recv, recvx, docs_in, res, resx, kt, vt, s0, dp0, e_own, dp_own, stat, ot0, dqt0, dkv,
    send_crosses, send_back,
):
    bf16, f32 = jnp.bfloat16, jnp.float32
    scale = SCORE_SCALE * LOG2_E
    eye = (iota((HD, HD), 0) == iota((HD, HD), 1)).astype(bf16)
    eye_block = (iota((BLOCK, BLOCK), 0) == iota((BLOCK, BLOCK), 1)).astype(bf16)
    q_all = [tile_rows(recv, t) for t in Q_OF]
    k_all = [tile_rows(recv, t) for t in K_OF]
    v_all = [tile_rows(recv, t) for t in V_OF]
    g_all = [tile_rows(recv, t) for t in D_OF]
    for kind in (0, 1):
        kt[kind] = dot_nt(eye, k_all[kind]).astype(bf16)
        vt[kind] = dot_nt(eye, v_all[kind]).astype(bf16)
    docs = [class_docs(docs_in, GROUP * half, (head + FINEST * kind) & (CLASSES - 1)) for kind in (0, 1)]
    cols = [d[0] for d in docs]
    q_docs = [d[1][0:1] for d in docs]

    stat[0] = jnp.full((8, SEG_ROWS), MASKED, f32)
    stat[1] = jnp.zeros((8, SEG_ROWS), f32)
    stat[2] = jnp.zeros((8, SEG_ROWS), f32)
    ot0[...] = jnp.zeros_like(ot0)
    dqt0[...] = jnp.zeros_like(dqt0)

    @pl.when(half == 1)
    def _():
        col0, _ = class_docs(docs_in, 0, head)
        k0 = tile_rows(recvx, 0)
        kt[2] = dot_nt(eye, k0).astype(bf16)
        vt[2] = dot_nt(eye, tile_rows(recvx, 1)).astype(bf16)
        for c in range(0, SEG_ROWS, BLOCK):
            at = pl.ds(c, BLOCK)
            query = q_all[0][c : c + BLOCK]
            top = None
            for r in range(0, SEG_ROWS, BLOCK):
                doc = col0[r : r + BLOCK]
                s = dot_nt(k0[r : r + BLOCK], query) * scale
                allowed = jnp.concatenate([doc, doc], 1) == q_docs[0][:, c : c + BLOCK]
                s = jnp.where(allowed, s, MASKED)
                s0[pl.ds(r, BLOCK), at] = s
                t = jnp.max(s, 0, keepdims=True)
                top = t if top is None else jnp.maximum(top, t)
            stat[0, 0:1, at] = top

    lower = iota((HD, BLOCK), 0) - (iota((HD, BLOCK), 1) & (HD - 1))
    is_a = iota((HD, BLOCK), 1) < HD
    b_is_later = jnp.where(head < FINEST, 1, 0)
    in_order = [
        lower <= jnp.where(is_a, 0, b_is_later - 1),
        lower <= jnp.where(is_a, -b_is_later, 0),
    ]
    bonus = jnp.where(iota((1, BLOCK), 1) < HD, 1.0, 0.0)
    both = lambda pair, i: jnp.concatenate([pair[0][i * HD : (i + 1) * HD], pair[1][i * HD : (i + 1) * HD]], 0)
    lanes = lambda pair, i: jnp.concatenate([pair[0][:, i * HD : (i + 1) * HD], pair[1][:, i * HD : (i + 1) * HD]], 1)
    blocks = SEG_ROWS // HD
    qs = [both(q_all, i) for i in range(blocks)]
    gs = [both(g_all, i) for i in range(blocks)]
    totals, drops = [], []
    for i in range(blocks):
        query_docs = lanes(q_docs, i)
        at = pl.ds(i * HD, HD)
        top = jnp.concatenate([stat[0, 0:1, at], jnp.full((1, HD), MASKED, f32)], 1)
        for kind in (0, 1):
            for t in range(i + 1):
                rows = slice(t * HD, (t + 1) * HD)
                s = dot_nt(k_all[kind][rows], qs[i]) * scale
                if kind == 0:
                    s = s + bonus
                doc = cols[kind][rows]
                allowed = jnp.concatenate([doc, doc], 1) == query_docs
                if t == i:
                    allowed = allowed & in_order[kind]
                s = jnp.where(allowed, s, MASKED)
                e_own[i, kind, rows] = s
                top = jnp.maximum(top, jnp.max(s, 0, keepdims=True))
        stat[0, 0:1, at] = top[:, :HD]
        total = jnp.zeros((1, BLOCK), f32)
        drop = jnp.zeros((1, BLOCK), f32)
        for kind in (0, 1):
            for t in range(i + 1):
                rows = slice(t * HD, (t + 1) * HD)
                e = jnp.exp2(e_own[i, kind, rows] - top)
                dp = dot_nt(v_all[kind][rows], gs[i])
                total = total + jnp.sum(e, 0, keepdims=True)
                drop = drop + jnp.sum(e * dp, 0, keepdims=True)
                e_own[i, kind, rows] = e
                dp_own[i, kind, rows] = dp
        totals.append(total)
        drops.append(drop)
    for i in range(blocks):
        at = pl.ds(i * HD, HD)
        stat[1, 0:1, at] = totals[i][:, :HD]
        stat[2, 0:1, at] = drops[i][:, :HD]

    @pl.when(half == 1)
    def _():
        v0 = tile_rows(recvx, 1)
        dk, dv = None, None
        for c in range(0, SEG_ROWS, BLOCK):
            at = pl.ds(c, BLOCK)
            query, grad = q_all[0][c : c + BLOCK], g_all[0][c : c + BLOCK]
            top = stat[0, 0:1, at]
            total, drop = stat[1, 0:1, at], stat[2, 0:1, at]
            for r in range(0, SEG_ROWS, BLOCK):
                rows = pl.ds(r, BLOCK)
                e = jnp.exp2(s0[rows, at] - top)
                dp = dot_nt(v0[r : r + BLOCK], grad)
                total = total + jnp.sum(e, 0, keepdims=True)
                drop = drop + jnp.sum(e * dp, 0, keepdims=True)
                s0[rows, at] = e
                dp0[rows, at] = dp
            stat[1, 0:1, at] = total
            stat[2, 0:1, at] = drop
            inverse = 1.0 / total
            drop = drop * inverse
            for r in range(0, SEG_ROWS, BLOCK):
                rows = pl.ds(r, BLOCK)
                w = s0[rows, at] * inverse
                ds = (w * (dp0[rows, at] - drop)).astype(bf16)
                w = w.astype(bf16)
                ot0[:, at] += dot_nn(vt[2, :, rows], w)
                dqt0[:, at] += dot_nn(kt[2, :, rows], ds)
                dk, dv = dot_nn(ds, query), dot_nn(w, grad)
                if c:
                    dk = dk + dkv[0, 2, rows]
                    dv = dv + dkv[1, 2, rows]
                dkv[0, 2, rows] = dk
                dkv[1, 2, rows] = dv
        resx[:, :ROWS] = (dkv[0, 2] * SCORE_SCALE).astype(bf16).reshape(GROUP, ROWS, HD)
        resx[:, ROWS:] = dkv[1, 2].astype(bf16).reshape(GROUP, ROWS, HD)
        send_crosses()

    for i in (0, 3, 2, 1):
        at = pl.ds(i * HD, HD)
        n = (i + 1) * HD
        total = jnp.concatenate([stat[1, 0:1, at], totals[i][:, HD:]], 1)
        drop = jnp.concatenate([stat[2, 0:1, at], drops[i][:, HD:]], 1)
        inverse = 1.0 / total
        drop = drop * inverse
        out_t = jnp.concatenate([ot0[:, at], jnp.zeros((HD, HD), f32)], 1)
        dq_t = jnp.concatenate([dqt0[:, at], jnp.zeros((HD, HD), f32)], 1)
        for kind in (0, 1):
            w = e_own[i, kind, :n] * inverse
            ds = (w * (dp_own[i, kind, :n] - drop)).astype(bf16)
            w = w.astype(bf16)
            out_t = out_t + dot_nn(vt[kind, :, :n], w)
            dq_t = dq_t + dot_nn(kt[kind, :, :n], ds)
            dk, dv = dot_nn(ds, qs[i]), dot_nn(w, gs[i])
            done = {0: 0, 3: HD, 2: n, 1: n}[i]
            for which, part in enumerate((dk, dv)):
                if done:
                    dkv[which, kind, :done] += part[:done]
                if done < n:
                    dkv[which, kind, done:n] = part[done:]
        out = dot_nt(eye_block, out_t.astype(bf16)).astype(bf16)
        dq = dot_nt(eye_block, (dq_t * SCORE_SCALE).astype(bf16)).astype(bf16)
        owners = slice(8 * i, 8 * i + 8)
        for kind in (0, 1):
            rows = slice(kind * HD, (kind + 1) * HD)
            for t, tile in enumerate((out[rows], dq[rows])):
                slot = (2 * t + kind) * ROWS
                res[owners, slot : slot + ROWS] = tile.reshape(8, ROWS, HD)
        if i:
            store_keys(dkv, res, i)
            send_back(i, 0, 8 * ROWS)
        else:
            send_back(i, 0, 4 * ROWS)
    store_keys(dkv, res, 0)
    send_back(0, 4 * ROWS, 4 * ROWS)


def store_keys(dkv, res, block):
    at = pl.ds(block * HD, HD)
    owners = slice(8 * block, 8 * block + 8)
    for kind in (0, 1):
        for t, tile in enumerate((dkv[0, kind, at] * SCORE_SCALE, dkv[1, kind, at])):
            slot = (4 + 2 * t + kind) * ROWS
            res[owners, slot : slot + ROWS] = tile.astype(jnp.bfloat16).reshape(8, ROWS, HD)


def place_kernel(back, backx, o_hbm, dq_hbm, dk_hbm, dv_hbm, rows_out, sems):
    first = lax.axis_index("seq") < GROUP
    copies = []
    for i, ref in enumerate((o_hbm, dq_hbm, dk_hbm, dv_hbm)):
        for h in range(H):
            shape = (TOKENS, 2 * ROWS)
            rank = iota(shape, 1)
            kind = (h + FINEST * (rank >> 4)) & (CLASSES - 1)
            spread = (iota(shape, 0) == CLASSES * (rank & (ROWS - 1)) + kind).astype(jnp.bfloat16)
            rows = back[h, 2 * i * ROWS : (2 * i + 2) * ROWS]
            if i >= 2:
                extra = backx[h, (i - 2) * ROWS : (i - 1) * ROWS].astype(jnp.float32)
                summed = rows[:ROWS].astype(jnp.float32) + jnp.where(first, extra, 0.0)
                rows = jnp.concatenate([summed.astype(jnp.bfloat16), rows[ROWS:]], 0)
            rows_out[i, :, h * HD : (h + 1) * HD] = dot_nn(spread, rows).astype(jnp.bfloat16)
        copies.append(pltpu.make_async_copy(rows_out.at[i], ref, sems.at[i]))
        copies[-1].start()
    for copy in copies:
        copy.wait()


def per_device(queries, keys, values, cotangent, doc_ids):
    any_space = pl.BlockSpec(memory_space=pl.ANY)
    vmem = pl.BlockSpec(memory_space=pltpu.VMEM)
    bf16, f32 = jnp.bfloat16, jnp.float32
    dma = pltpu.SemaphoreType.DMA
    back, backx = pl.pallas_call(
        exchange_kernel,
        out_shape=(
            jax.ShapeDtypeStruct((H, 8 * ROWS, HD), bf16),
            jax.ShapeDtypeStruct((H, 2 * ROWS, HD), bf16),
        ),
        in_specs=[any_space] * 5,
        out_specs=(any_space, any_space),
        scratch_shapes=[
            pltpu.VMEM((1, TOKENS), jnp.int32),
            pltpu.VMEM((SEQ_DEVICES, 1, TOKENS), jnp.int32),
            pltpu.VMEM((4, TOKENS, H * HD), bf16),
            pltpu.VMEM((H, MESSAGE, HD), bf16),
            pltpu.VMEM((GROUP, MESSAGE, HD), bf16),
            pltpu.VMEM((GROUP, CROSS, HD), bf16),
            pltpu.VMEM((GROUP, 8 * ROWS, HD), bf16),
            pltpu.VMEM((GROUP, 2 * ROWS, HD), bf16),
            pltpu.VMEM((3, HD, SEG_ROWS), bf16),
            pltpu.VMEM((3, HD, SEG_ROWS), bf16),
            pltpu.VMEM((SEG_ROWS, SEG_ROWS), f32),
            pltpu.VMEM((SEG_ROWS, SEG_ROWS), f32),
            pltpu.VMEM((SEG_ROWS // HD, 2, SEG_ROWS, BLOCK), f32),
            pltpu.VMEM((SEG_ROWS // HD, 2, SEG_ROWS, BLOCK), f32),
            pltpu.VMEM((3, 8, SEG_ROWS), f32),
            pltpu.VMEM((HD, SEG_ROWS), f32),
            pltpu.VMEM((HD, SEG_ROWS), f32),
            pltpu.VMEM((2, 3, SEG_ROWS, HD), f32),
            dma((5,)),
            dma,
            dma,
            dma,
            dma,
            dma,
            dma,
            dma,
        ],
        compiler_params=pltpu.CompilerParams(
            collective_id=0, has_side_effects=True, vmem_limit_bytes=28 * 2**20
        ),
        name="exchange",
    )(*[pltpu.with_memory_space_constraint(a, pltpu.HBM) for a in (queries, keys, values, cotangent, doc_ids.reshape(1, TOKENS))])
    full = jax.ShapeDtypeStruct((TOKENS, H * HD), bf16)
    return tuple(
        pl.pallas_call(
            place_kernel,
            out_shape=(full,) * 4,
            in_specs=[vmem, vmem],
            out_specs=(any_space,) * 4,
            scratch_shapes=[pltpu.VMEM((4, TOKENS, H * HD), bf16), dma((4,))],
            compiler_params=pltpu.CompilerParams(vmem_limit_bytes=16 * 2**20),
            name="place",
        )(back, backx)
    )


def solution(mesh):
    spec = P(("dp", "seq"), None)
    return jax.shard_map(
        per_device,
        mesh=mesh,
        in_specs=(spec, spec, spec, spec, P(("dp", "seq"))),
        out_specs=(spec,) * 4,
        check_vma=False,
    )
```
